32 devices in a mesh: grp: 2 (over y), loan: 4 (over z), feat: 4 (over x, core).
Axes of the slice: x: 2, y: 2, z: 4, core: 2. Of those that a mesh axis runs over, the one named last changes fastest.
Arguments:
- design: bfloat16 [16384, 4096], P(('grp', 'loan'), 'feat'), parts along dimension 0, may hold values from -6 to 6
- labels: int32 [16384], P(('grp', 'loan')), parts along dimension 0, may hold values from 0 to 1
- pool_ids: int32 [16384], P(('grp', 'loan')), parts along dimension 0, may hold values from 0 to 255, as said below
- pool_region_index: int32 [512], P(('grp', 'loan')), parts along dimension 0, may hold values from 0 to 63
- step_size: float32 [32], P('grp'), parts along dimension 0, may hold values from 0.005 to 0.02
- beta: float32 [32, 4096], P('grp', 'feat'), parts along dimension 0, may hold values from -0.09375 to 0.09375
- pools: float32 [32, 256, 256], P('grp', 'loan', 'feat'), parts along dimension 0, may hold values from -0.5 to 0.5
- regions: float32 [32, 64, 256], P('grp', None, 'feat'), parts along dimension 0, may hold values from -0.5 to 0.5
- beta_momentum: float32 [32, 4096], P('grp', 'feat'), parts along dimension 0, may hold values from -6 to 6
- pool_momentum: float32 [32, 256, 256], P('grp', 'loan', 'feat'), parts along dimension 0, may hold values from -6 to 6
- region_momentum: float32 [32, 64, 256], P('grp', None, 'feat'), parts along dimension 0, may hold values from -6 to 6
Outputs:
- beta_next: float32 [32, 4096], P('grp', 'feat'), parts along dimension 0
- pools_next: float32 [32, 256, 256], P('grp', 'loan', 'feat'), parts along dimension 0
- regions_next: float32 [32, 64, 256], P('grp', None, 'feat'), parts along dimension 0
- beta_momentum_next: float32 [32, 4096], P('grp', 'feat'), parts along dimension 0
- pool_momentum_next: float32 [32, 256, 256], P('grp', 'loan', 'feat'), parts along dimension 0
- region_momentum_next: float32 [32, 64, 256], P('grp', None, 'feat'), parts along dimension 0
The draws below stay inside these ranges and needn't reach their ends.
There are 2 independent parts, one for each index of `grp`. The reference program is written for one: setup_inputs(seed, part) draws one part's arguments, and reference() takes and returns one part's arrays. A program takes and returns all parts, laid end to end along the dimension named above; each array names one. Nothing has to cross between parts.
Inputs may be any that keep to these rules, and one draw needn't show every extreme that they name: `pool_ids`: in each aligned block of 2048 loans (block l counted from 0) the pool ids lie in l * 64 to (l + 1) * 64 - 1 and do not fall along the block.
All inputs are finite; a program needn't handle non-finite values.
Results may differ from the reference program's by a relative error of at most 0.0006.
Values may be sent and summed in bfloat16 or wider, within the bound.
A program may use at most 64 MiB of HBM per device.

```python
import math
import jax
import jax.numpy as jnp
from jax import lax

F = 4096
G = 256
R = 64
CHAINS = 16
ROWS_DEV = 2048
POOLS_DEV = 64
LOANS = 8192
POOLS = 256
N_LOAN = 4


def draw_pool_ids(key, part):
    blocks = jax.random.randint(key, (N_LOAN, ROWS_DEV), 0, POOLS_DEV)
    blocks = jnp.sort(blocks, axis=1) + jnp.arange(N_LOAN, dtype=jnp.int32)[:, None] * POOLS_DEV
    return blocks.reshape(-1).astype(jnp.int32)


def plant(entries, stream_key, low, high):
    index_at = [jax.random.randint(jax.random.fold_in(stream_key, axis), (), 0, length) for axis, length in enumerate(entries.shape)]
    longest = entries.shape.index(max(entries.shape))
    beside = index_at[:longest] + [(index_at[longest] + 1) % entries.shape[longest]] + index_at[longest + 1:]
    return entries.at[tuple(index_at)].set(low).at[tuple(beside)].set(high)


def steps_of(key, shape, pieces, low, top_value):
    level, own = 1.0, jax.random.fold_in(key, 6)
    for axis_at, blocks in pieces:
        draws = jnp.exp(jax.random.uniform(jax.random.fold_in(own, axis_at), (blocks,), jnp.float32, low / len(pieces), top_value / len(pieces)))
        level = level * jnp.repeat(draws, shape[axis_at] // blocks).reshape([-1 if axis == axis_at else 1 for axis in range(len(shape))])
    return level


def noise(rng, dims, spread, bound, cuts=(), kind=jnp.bfloat16):
    factor_of = steps_of(rng, dims, cuts, -0.22, 0.18) if cuts else 1.0
    drawn = jax.random.normal(rng, dims, jnp.float32) * spread * factor_of
    return jnp.minimum(jnp.maximum(drawn, -bound), bound).astype(kind)


def setup_inputs(seed: int = 0, part: int = 0) -> dict:
    key_of = jax.random.split(jax.random.key(seed), 12)
    part_splits = jax.random.split(jax.random.fold_in(key_of[11], part), 12)
    return {
        "design": noise(part_splits[0], (LOANS, F), 1.0, 6.0, ((0, 4), (1, 4))),
        "labels": plant(jax.random.randint(part_splits[1], (LOANS,), 0, 2), jax.random.fold_in(part_splits[1], 1), 0, 1).astype(jnp.int32),
        "pool_ids": draw_pool_ids(jax.random.fold_in(jax.random.fold_in(key_of[11], part), 71), part),
        "pool_region_index": plant(jax.random.randint(part_splits[3], (POOLS,), 0, R), jax.random.fold_in(part_splits[3], 1), 0, R - 1).astype(jnp.int32),
        "step_size": jnp.clip(jnp.exp(jax.random.uniform(part_splits[4], (CHAINS,), jnp.float32, math.log(0.005), math.log(0.02))), 0.005, 0.02),
        "beta": noise(part_splits[5], (CHAINS, F), F ** -0.5, 0.09375, ((1, 4),), jnp.float32),
        "pools": noise(part_splits[6], (CHAINS, POOLS, G), 0.0625, 0.5, ((1, 4), (2, 4)), jnp.float32),
        "regions": noise(part_splits[7], (CHAINS, R, G), 0.0625, 0.5, ((2, 4),), jnp.float32),
        "beta_momentum": noise(part_splits[8], (CHAINS, F), 1.0, 6.0, ((1, 4),), jnp.float32),
        "pool_momentum": noise(part_splits[9], (CHAINS, POOLS, G), 1.0, 6.0, ((1, 4), (2, 4)), jnp.float32),
        "region_momentum": noise(part_splits[10], (CHAINS, R, G), 1.0, 6.0, ((2, 4),), jnp.float32),
    }


MATMUL_ACCURACY = 256.0


def gradient(design, labels, pool_ids, pool_region_index, b, upper_operand, lower_operand):
    stride = F // G
    slope_feats = design[:, ::stride].astype(jnp.float32)
    b16 = b.astype(jnp.bfloat16)
    linear = lax.dot_general(b16, design, (((1,), (1,)), ((), ())), preferred_element_type=jnp.float32)
    term = lax.map(lambda uc: jnp.sum(slope_feats * uc[pool_ids], axis=1), upper_operand)
    logit = linear + term
    resid = (labels.astype(jnp.float32)[None, :] - jax.nn.sigmoid(logit)).astype(jnp.bfloat16)
    xt = lax.dot_general(resid, design, (((1,), (0,)), ((), ())), preferred_element_type=jnp.float32)
    gb = xt - F * b
    rf = resid.astype(jnp.float32)
    lik = lax.map(lambda rc: jax.ops.segment_sum(slope_feats * rc[:, None], pool_ids, num_segments=POOLS), rf)
    selected_operand = lower_operand[:, pool_region_index, :]
    device_index = MATMUL_ACCURACY * (upper_operand - selected_operand)
    gu = lik - device_index
    sums = jax.ops.segment_sum(jnp.moveaxis(device_index, 1, 0), pool_region_index, num_segments=R)
    gv = jnp.moveaxis(sums, 0, 1) - MATMUL_ACCURACY * lower_operand
    return gb, gu, gv


def reference(design, labels, pool_ids, pool_region_index, step_size, beta, pools, regions, beta_momentum, pool_momentum, region_momentum):
    half = 0.5 * step_size
    h2 = half[:, None]
    h3 = half[:, None, None]
    e2 = step_size[:, None]
    e3 = step_size[:, None, None]
    gb, gu, gv = gradient(design, labels, pool_ids, pool_region_index, beta, pools, regions)
    mb = beta_momentum + h2 * gb
    mu = pool_momentum + h3 * gu
    mv = region_momentum + h3 * gv
    beta_next = beta + e2 * mb
    pools_next = pools + e3 * mu
    regions_next = regions + e3 * mv
    gb, gu, gv = gradient(design, labels, pool_ids, pool_region_index, beta_next, pools_next, regions_next)
    return beta_next, pools_next, regions_next, mb + h2 * gb, mu + h3 * gu, mv + h3 * gv
```

```python
import functools

import jax
import jax.numpy as jnp
from jax import lax
from jax.experimental import pallas as pl
from jax.experimental.pallas import tpu as pltpu
from jax.sharding import PartitionSpec as P

PREC = 256.0
MESH = pl.DeviceIdType.MESH
NT = (((1,), (1,)), ((), ()))
NN = (((1,), (0,)), ((), ()))
F32 = jnp.float32
BF16 = jnp.bfloat16


def dot(a, b, dims=NN):
    return lax.dot_general(a, b, dims, preferred_element_type=F32)


def halves(x):
    hi = x.astype(BF16)
    return hi, (x - hi.astype(F32)).astype(BF16)


def blocks_of(owned, g_own):
    return max(1, min(256 // g_own, owned // 16))


def kernel(
    nf,
    nl,
    design_hbm,
    labels_hbm,
    ids_hbm,
    pri_hbm,
    step_hbm,
    beta_hbm,
    pools_hbm,
    regions_hbm,
    beta_m_hbm,
    pool_m_hbm,
    region_m_hbm,
    beta_n,
    pools_n,
    regions_n,
    beta_mn,
    pool_mn,
    region_mn,
    design,
    labels,
    ids,
    pri,
    step_s,
    beta,
    pools,
    regions,
    beta_m,
    pool_m,
    region_m,
    lhs,
    mask,
    fold,
    u4,
    lik,
    term,
    dev,
    part,
    rs_buf,
    resid,
    resid_f,
    xt_buf,
    reg_part,
    reg_buf,
    reg_all,
    load,
    load_d,
    s_rs,
    r_rs,
    s_ag,
    r_ag,
    s_xt,
    r_xt,
    s_rr,
    r_rr,
    s_ra,
    r_ra,
    s_pr,
    r_pr,
):
    fi = lax.axis_index("feat")
    li = lax.axis_index("loan")
    chains, owned, g_own = pools.shape
    feats = beta.shape[1]
    n_reg = regions.shape[1]
    width = labels.shape[2]
    stride = feats // g_own
    total_feats = float(feats * nf)
    nb = blocks_of(owned, g_own)
    prow = owned // nb
    lanes = chains * g_own
    side = max(1, 128 // g_own)
    span = side * g_own
    nx = nf // 2
    order = [k for k in range(2, nf)] + [1, 0]
    arrive = [0, 1] + [k for k in range(2, nf)]

    def peer_of(k):
        return lax.rem(fi // 2 + k // 2, nx) * 2 + lax.rem(fi + k, 2)

    def source_of(k):
        return lax.rem(fi // 2 + nx - k // 2, nx) * 2 + lax.rem(fi + k, 2)

    def fetch_rows(k):
        j = peer_of(k)
        return pltpu.make_async_copy(
            design_hbm.at[pl.ds(pl.multiple_of(j * width, width), width), :],
            design.at[j],
            load_d.at[k],
        )

    def fetch(i):
        src, dst = (
            (beta_hbm, beta),
            (ids_hbm, ids),
            (pools_hbm, pools),
            (labels_hbm, labels),
            (pri_hbm, pri.at[li]),
            (step_hbm, step_s),
            (regions_hbm, regions),
            (pool_m_hbm, pool_m),
            (region_m_hbm, region_m),
            (beta_m_hbm, beta_m),
        )[i]
        return pltpu.make_async_copy(src, dst, load.at[i])

    for i in range(2):
        fetch(i).start()
    fetch_rows(order[0]).start()
    fetch(2).start()
    for k in order[1:]:
        fetch_rows(k).start()
    for i in range(3, 10):
        fetch(i).start()

    barrier = pltpu.get_barrier_semaphore()
    for k in range(1, nf):
        pl.semaphore_signal(
            barrier, inc=1, device_id={"feat": peer_of(k)}, device_id_type=MESH
        )
    for k in range(1, nl):
        pl.semaphore_signal(
            barrier, inc=1, device_id={"loan": lax.rem(li + k, nl)}, device_id_type=MESH
        )

    def remote(src, dst, ss, rs, axis, peer):
        return pltpu.make_async_remote_copy(
            src_ref=src,
            dst_ref=dst,
            send_sem=ss,
            recv_sem=rs,
            device_id={axis: peer},
            device_id_type=MESH,
        )

    def rs_copy(t, k):
        peer = peer_of(k)
        return remote(
            part.at[t, peer], rs_buf.at[t, k - 1], s_rs.at[t, k - 1], r_rs.at[t, k - 1], "feat", peer
        )

    def ag_copy(t, k, slot):
        return remote(
            resid.at[t, slot],
            resid.at[t, slot],
            s_ag.at[t, k - 1],
            r_ag.at[t, k - 1],
            "feat",
            peer_of(k),
        )

    def loan_peer(k):
        return lax.rem(li + k, nl)

    def loan_source(k):
        return lax.rem(li + nl - k, nl)

    def xt_copy(t, k):
        return remote(
            xt_buf.at[t, 0],
            xt_buf.at[t, k],
            s_xt.at[t, k - 1],
            r_xt.at[t, k - 1],
            "loan",
            loan_peer(k),
        )

    def rr_copy(t, k):
        peer = loan_peer(k)
        return remote(
            reg_part.at[t, peer], reg_buf.at[t, k - 1], s_rr.at[t, k - 1], r_rr.at[t, k - 1], "loan", peer
        )

    def ra_copy(t, k, owner):
        return remote(
            reg_all.at[t, owner],
            reg_all.at[t, owner],
            s_ra.at[t, k - 1],
            r_ra.at[t, k - 1],
            "loan",
            loan_peer(k),
        )

    def pr_copy(k, owner):
        return remote(
            pri.at[owner], pri.at[owner], s_pr.at[k - 1], r_pr.at[k - 1], "loan", loan_peer(k)
        )

    def onehot_t(row):
        return (row == lax.broadcasted_iota(jnp.int32, (n_reg, owned), 0)).astype(F32)

    def wide(ref, i):
        return jnp.concatenate([ref[i * side + c] for c in range(side)], axis=1)

    def cols(i):
        return pl.ds(i * span, span)

    n_cols = lanes // span

    def prologue():
        fetch(0).wait()
        lhs[pl.ds(0, chains), :] = beta[...].astype(BF16)
        lhs[pl.ds(chains, g_own), :] = (
            (
                lax.broadcasted_iota(jnp.int32, (g_own, feats), 1)
                == stride * lax.broadcasted_iota(jnp.int32, (g_own, feats), 0)
            )
            .astype(F32)
            .astype(BF16)
        )
        fetch(1).wait()

    def put_u4(c, blocks):
        hi, lo = halves(jnp.concatenate(blocks, axis=1))
        u4[pl.ds(c * prow, prow), :] = hi
        u4[pl.ds((chains + c) * prow, prow), :] = lo

    def slopes_first():
        fetch(2).wait()
        for c in range(chains):
            put_u4(c, [pools[c, pl.ds(k * prow, prow), :] for k in range(nb)])

    def slopes_next():
        for c in range(chains):
            put_u4(
                c,
                [
                    pools_n[pl.ds(k * prow, prow), pl.ds(c * g_own, g_own)]
                    for k in range(nb)
                ],
            )

    def pool_term(j):
        z = dot(u4[...], fold[j])
        m = mask[j]
        low = chains * prow
        for c in range(chains):
            a = z[c * prow : (c + 1) * prow] + z[low + c * prow : low + (c + 1) * prow]
            term[j, pl.ds(c, 1), :] = jnp.sum(a * m, axis=0, keepdims=True)

    first = li * owned

    def logits_first(k):
        j = peer_of(k)
        fetch_rows(k).wait()
        both = dot(lhs[...], design[j], NT)
        local = ids[j] - first
        block = local // prow
        mask[j] = (
            local - block * prow == lax.broadcasted_iota(jnp.int32, (prow, width), 0)
        ).astype(F32)
        slope = both[chains:]
        for b in range(nb):
            fold[j, pl.ds(b * g_own, g_own), :] = jnp.where(block == b, slope, 0.0).astype(BF16)
        pool_term(j)
        part[0, j] = term[j] + both[:chains]
        if k:
            rs_copy(0, k).start()

    def terms_next():
        def chunk(j, carry):
            pool_term(j)
            return carry

        lax.fori_loop(0, nf, chunk, 0)

    def logits_next():
        b16 = beta_n[...].astype(BF16)
        for k in order:
            j = peer_of(k)
            part[1, j] = term[j] + dot(b16, design[j], NT)
            if k:
                rs_copy(1, k).start()

    def residuals(t):
        logit = part[t, fi]
        for k in range(1, nf):
            rs_copy(t, k).wait_recv()
            logit = logit + rs_buf[t, k - 1]
        mine = (labels[fi].astype(F32) - jax.nn.sigmoid(logit)).astype(BF16)
        resid[t, fi] = mine
        for k in order[:-1]:
            ag_copy(t, k, fi).start()

    def population(t, k):
        s = source_of(k)
        if k:
            ag_copy(t, k, s).wait_recv()
        x = dot(resid[t, s], design[s])
        if k == arrive[0]:
            xt_buf[t, 0] = x
        else:
            xt_buf[t, 0] += x

    def population_send(t):
        for k in range(1, nl):
            xt_copy(t, k).start()

    def population_sum(t):
        for k in range(1, nl):
            xt_copy(t, k).wait_recv()
        total = xt_buf[t, li]
        for j in range(1, nl):
            total = total + xt_buf[t, lax.rem(li + nl - j, nl)]
        return total

    def likelihood(t, k):
        s = source_of(k)
        resid_f[...] = resid[t, s].astype(F32)
        m = mask[s]
        a = jnp.concatenate(
            [(resid_f[pl.ds(c, 1), :] * m).astype(BF16) for c in range(chains)], axis=0
        )
        x = dot(a, fold[s], NT)
        if k == arrive[0]:
            lik[...] = x
        else:
            lik[...] += x

    def lik_cols(i):
        return jnp.concatenate(
            [
                jnp.concatenate(
                    [
                        lik[
                            pl.ds((i * side + c) * prow, prow), pl.ds(k * g_own, g_own)
                        ]
                        for c in range(side)
                    ],
                    axis=1,
                )
                for k in range(nb)
            ],
            axis=0,
        )

    def step_cols(i):
        lane = lax.broadcasted_iota(jnp.int32, (1, span), 1) // g_own
        e = jnp.zeros((1, span), F32)
        for c in range(side):
            e = jnp.where(lane == c, step_s[i * side + c], e)
        return e

    def region_sum(t, get):
        oht = onehot_t(pri[li])
        oht2 = jnp.concatenate([oht, oht], axis=1).astype(BF16)
        rows = n_reg // nl
        for i in range(n_cols):
            hi, lo = halves(get(i))
            s = dot(oht2, jnp.concatenate([hi, lo], axis=0))
            for o in range(nl):
                reg_part[t, o, :, cols(i)] = s[o * rows : (o + 1) * rows]

    def region_send(t):
        for k in range(1, nl):
            rr_copy(t, k).start()

    def deviation(get_u, get_v):
        oht = onehot_t(pri[li])
        eye = (
            lax.broadcasted_iota(jnp.int32, (owned, owned), 0)
            == lax.broadcasted_iota(jnp.int32, (owned, owned), 1)
        ).astype(F32)
        oh = dot(eye.astype(BF16), oht.astype(BF16), NT)
        oh2 = jnp.concatenate([oh, oh], axis=1).astype(BF16)
        for i in range(n_cols):
            hi, lo = halves(get_v(i))
            dev[:, cols(i)] = PREC * (get_u(i) - dot(oh2, jnp.concatenate([hi, lo], axis=0)))

    def region_first():
        fetch(4).wait()
        region_sum(0, lambda i: wide(pools, i))
        for k in range(1, nl):
            pr_copy(k, li).start()
        region_send(0)

    def deviation_first():
        fetch(6).wait()
        deviation(lambda i: wide(pools, i), lambda i: wide(regions, i))

    def region_reduce(t):
        total = reg_part[t, li]
        for k in range(1, nl):
            rr_copy(t, k).wait_recv()
            total = total + reg_buf[t, k - 1]
        reg_all[t, li] = total
        for k in range(1, nl):
            ra_copy(t, k, li).start()

    def region_gather(t):
        for k in range(1, nl):
            ra_copy(t, k, loan_source(k)).wait_recv()

    def counts():
        n = jnp.zeros((n_reg, 1), F32)
        for i in range(nl):
            n = n + jnp.sum(onehot_t(pri[i]), axis=1, keepdims=True)
        return n + 1.0

    def region_force(t, i, get_v, n):
        s = jnp.concatenate([reg_all[t, o, :, cols(i)] for o in range(nl)], axis=0)
        return PREC * (s - n * get_v(i))

    def wait_rest():
        fetch(3).wait()
        fetch(5).wait()

    def pool_update():
        fetch(7).wait()
        for i in range(n_cols):
            e = step_cols(i)
            m = wide(pool_m, i) + (0.5 * e) * (lik_cols(i) - dev[:, cols(i)])
            pool_mn[:, cols(i)] = m
            pools_n[:, cols(i)] = wide(pools, i) + e * m

    def region_next():
        fetch(8).wait()
        region_gather(0)
        for k in range(1, nl):
            pr_copy(k, loan_source(k)).wait_recv()
        n = counts()
        for i in range(n_cols):
            e = step_cols(i)
            g = region_force(0, i, lambda i: wide(regions, i), n)
            m = wide(region_m, i) + (0.5 * e) * g
            region_mn[:, cols(i)] = m
            regions_n[:, cols(i)] = wide(regions, i) + e * m
        deviation(lambda i: pools_n[:, cols(i)], lambda i: regions_n[:, cols(i)])

    def region_last():
        region_gather(1)
        n = counts()
        for i in range(n_cols):
            g = region_force(1, i, lambda i: regions_n[:, cols(i)], n)
            region_mn[:, cols(i)] += (0.5 * step_cols(i)) * g

    def pool_last():
        for i in range(n_cols):
            pool_mn[:, cols(i)] += (0.5 * step_cols(i)) * (lik_cols(i) - dev[:, cols(i)])

    def step_rows():
        chain = lax.broadcasted_iota(jnp.int32, (chains, 1), 0)
        e = jnp.zeros((chains, 1), F32)
        for c in range(chains):
            e = jnp.where(chain == c, step_s[c], e)
        return e

    def beta_next():
        fetch(9).wait()
        e = step_rows()
        m = beta_m[...] + (0.5 * e) * (population_sum(0) - total_feats * beta[...])
        beta_mn[...] = m
        beta_n[...] = beta[...] + e * m

    def beta_last():
        beta_mn[...] += (0.5 * step_rows()) * (population_sum(1) - total_feats * beta_n[...])

    def barrier_wait():
        pl.semaphore_wait(barrier, nf + nl - 2)

    def sum_next():
        region_sum(1, lambda i: pools_n[:, cols(i)])
        region_send(1)

    def sent():
        for t in range(2):
            for k in range(1, nf):
                rs_copy(t, k).wait_send()
                ag_copy(t, k, fi).wait_send()
            for k in range(1, nl):
                xt_copy(t, k).wait_send()
                rr_copy(t, k).wait_send()
                ra_copy(t, k, li).wait_send()
        for k in range(1, nl):
            pr_copy(k, li).wait_send()

    prologue()
    slopes_first()
    barrier_wait()
    for k in order:
        logits_first(k)
    region_first()
    deviation_first()
    wait_rest()
    residuals(0)
    for k in arrive[:2]:
        population(0, k)
        likelihood(0, k)
    region_reduce(0)
    for k in arrive[2:]:
        population(0, k)
    population_send(0)
    for k in arrive[2:]:
        likelihood(0, k)
    pool_update()
    slopes_next()
    terms_next()
    sum_next()
    beta_next()
    logits_next()
    region_next()
    residuals(1)
    for k in arrive[:2]:
        population(1, k)
        likelihood(1, k)
    region_reduce(1)
    for k in arrive[2:]:
        population(1, k)
    population_send(1)
    for k in arrive[2:]:
        likelihood(1, k)
    pool_last()
    region_last()
    beta_last()
    sent()


def emit(
    beta_n,
    pools_n,
    regions_n,
    beta_mn,
    pool_mn,
    region_mn,
    beta_o,
    pools_o,
    regions_o,
    beta_mo,
    pool_mo,
    region_mo,
    pools_v,
    regions_v,
    pool_mv,
    region_mv,
    sem,
):
    pending = [
        pltpu.make_async_copy(beta_n, beta_o, sem.at[0]),
        pltpu.make_async_copy(beta_mn, beta_mo, sem.at[1]),
    ]
    for copy in pending:
        copy.start()
    wide = (
        (pools_n, pools_v, pools_o),
        (regions_n, regions_v, regions_o),
        (pool_mn, pool_mv, pool_mo),
        (region_mn, region_mv, region_mo),
    )
    for n, (src, tmp, dst) in enumerate(wide):
        chains, _, g_own = tmp.shape
        for c in range(chains):
            tmp[c] = src[:, pl.ds(c * g_own, g_own)]
        copy = pltpu.make_async_copy(tmp, dst, sem.at[2 + n])
        copy.start()
        pending.append(copy)
    for copy in pending:
        copy.wait()


def body(
    nf,
    nl,
    design,
    labels,
    pool_ids,
    pool_region_index,
    step_size,
    beta,
    pools,
    regions,
    beta_momentum,
    pool_momentum,
    region_momentum,
):
    loans, feats = design.shape
    chains, owned, g_own = pools.shape
    n_reg = regions.shape[1]
    width = loans // nf
    lanes = chains * g_own
    nb = blocks_of(owned, g_own)
    prow = owned // nb
    rows = n_reg // nl
    vmem = pl.BlockSpec(memory_space=pltpu.VMEM)
    hbm = pl.BlockSpec(memory_space=pltpu.HBM)
    dma = pltpu.SemaphoreType.DMA
    args = (
        design,
        labels.reshape(nf, 1, width),
        pool_ids.reshape(nf, 1, width),
        pool_region_index.reshape(1, owned),
        step_size,
        beta,
        pools,
        regions,
        beta_momentum,
        pool_momentum,
        region_momentum,
    )
    outs = (beta, pools, regions, beta_momentum, pool_momentum, region_momentum)
    packed = tuple(
        OUT(x.shape if x.ndim == 2 else (x.shape[1], lanes), F32) for x in outs
    )
    results = pl.pallas_call(
        functools.partial(kernel, nf, nl),
        out_shape=packed,
        in_specs=[hbm] * len(args),
        out_specs=tuple(vmem for _ in outs),
        scratch_shapes=[
            pltpu.VMEM((nf, width, feats), BF16),
            pltpu.VMEM((nf, 1, width), jnp.int32),
            pltpu.VMEM((nf, 1, width), jnp.int32),
            pltpu.VMEM((nl, 1, owned), jnp.int32),
            pltpu.SMEM(step_size.shape, F32),
            pltpu.VMEM(beta.shape, F32),
            pltpu.VMEM(pools.shape, F32),
            pltpu.VMEM(regions.shape, F32),
            pltpu.VMEM(beta.shape, F32),
            pltpu.VMEM(pools.shape, F32),
            pltpu.VMEM(regions.shape, F32),
            pltpu.VMEM((chains + g_own, feats), BF16),
            pltpu.VMEM((nf, prow, width), F32),
            pltpu.VMEM((nf, nb * g_own, width), BF16),
            pltpu.VMEM((2 * chains * prow, nb * g_own), BF16),
            pltpu.VMEM((chains * prow, nb * g_own), F32),
            pltpu.VMEM((nf, chains, width), F32),
            pltpu.VMEM((owned, lanes), F32),
            pltpu.VMEM((2, nf, chains, width), F32),
            pltpu.VMEM((2, nf - 1, chains, width), F32),
            pltpu.VMEM((2, nf, chains, width), BF16),
            pltpu.VMEM((chains, width), F32),
            pltpu.VMEM((2, nl, chains, feats), F32),
            pltpu.VMEM((2, nl, rows, lanes), F32),
            pltpu.VMEM((2, nl - 1, rows, lanes), F32),
            pltpu.VMEM((2, nl, rows, lanes), F32),
            dma((10,)),
            dma((nf,)),
            dma((2, nf - 1)),
            dma((2, nf - 1)),
            dma((2, nf - 1)),
            dma((2, nf - 1)),
            dma((2, nl - 1)),
            dma((2, nl - 1)),
            dma((2, nl - 1)),
            dma((2, nl - 1)),
            dma((2, nl - 1)),
            dma((2, nl - 1)),
            dma((nl - 1,)),
            dma((nl - 1,)),
        ],
        compiler_params=pltpu.CompilerParams(
            collective_id=0, has_side_effects=True, vmem_limit_bytes=VLIM << 20
        ),
    )(*[pltpu.with_memory_space_constraint(x, pltpu.HBM) for x in args])
    return pl.pallas_call(
        emit,
        out_shape=tuple(jax.ShapeDtypeStruct(x.shape, x.dtype) for x in outs),
        in_specs=[vmem] * len(outs),
        out_specs=tuple(hbm for _ in outs),
        scratch_shapes=[
            pltpu.VMEM(pools.shape, F32),
            pltpu.VMEM(regions.shape, F32),
            pltpu.VMEM(pools.shape, F32),
            pltpu.VMEM(regions.shape, F32),
            dma((6,)),
        ],
        compiler_params=pltpu.CompilerParams(vmem_limit_bytes=16 << 20),
    )(*results)


VLIM = 24
OUT = pltpu.VMEM


def solution(mesh):
    in_specs = (
        P(("grp", "loan"), "feat"),
        P(("grp", "loan")),
        P(("grp", "loan")),
        P(("grp", "loan")),
        P("grp"),
        P("grp", "feat"),
        P("grp", "loan", "feat"),
        P("grp", None, "feat"),
        P("grp", "feat"),
        P("grp", "loan", "feat"),
        P("grp", None, "feat"),
    )
    out_specs = (
        P("grp", "feat"),
        P("grp", "loan", "feat"),
        P("grp", None, "feat"),
        P("grp", "feat"),
        P("grp", "loan", "feat"),
        P("grp", None, "feat"),
    )
    step = functools.partial(body, mesh.shape["feat"], mesh.shape["loan"])
    return jax.shard_map(step, mesh=mesh, in_specs=in_specs, out_specs=out_specs, check_vma=False)
```

```python
import functools

import jax
import jax.numpy as jnp
from jax import lax
from jax.experimental import pallas as pl
from jax.experimental.pallas import tpu as pltpu
from jax.sharding import PartitionSpec as P

PREC = 256.0
MESH = pl.DeviceIdType.MESH
NT = (((1,), (1,)), ((), ()))
NN = (((1,), (0,)), ((), ()))
F32 = jnp.float32
BF16 = jnp.bfloat16
I16 = jnp.int16
TOP = 32767.0


def dot(a, b, dims=NN):
    return lax.dot_general(a, b, dims, preferred_element_type=F32)


def halves(x):
    hi = x.astype(BF16)
    return hi, (x - hi.astype(F32)).astype(BF16)


def code(x):
    top = jnp.max(jnp.abs(x), axis=0, keepdims=True)
    top = jnp.maximum(top, 1e-30)
    q = jnp.round(x * (TOP / top)).astype(jnp.int32).astype(I16)
    return q, top * (1.0 / TOP)


def decode(q, scale):
    return q.astype(jnp.int32).astype(F32) * scale


def blocks_of(owned, g_own):
    return max(1, min(256 // g_own, owned // 16))


def kernel(
    nf,
    nl,
    design_hbm,
    labels_hbm,
    ids_hbm,
    pri_hbm,
    step_hbm,
    beta_hbm,
    pools_hbm,
    regions_hbm,
    beta_m_hbm,
    pool_m_hbm,
    region_m_hbm,
    beta_n,
    pools_n,
    regions_n,
    beta_mn,
    pool_mn,
    region_mn,
    design,
    labels,
    ids,
    pri,
    step_s,
    beta,
    pools,
    regions,
    beta_m,
    pool_m,
    region_m,
    lhs,
    mask,
    fold,
    u4,
    lik,
    term,
    dev,
    part,
    rs_buf,
    resid,
    resid_f,
    xt_f,
    xt_q,
    xt_s,
    part_q,
    part_s,
    buf_q,
    buf_s,
    all_q,
    all_s,
    flipped,
    eye,
    load,
    load_d,
    s_rs,
    r_rs,
    s_ag,
    r_ag,
    s_xt,
    r_xt,
    s_rr,
    r_rr,
    s_ra,
    r_ra,
    s_pr,
    r_pr,
):
    fi = lax.axis_index("feat")
    li = lax.axis_index("loan")
    chains, owned, g_own = pools.shape
    feats = beta.shape[1]
    n_reg = regions.shape[1]
    width = labels.shape[2]
    stride = feats // g_own
    total_feats = float(feats * nf)
    nb = blocks_of(owned, g_own)
    prow = owned // nb
    lanes = chains * g_own
    side = max(1, 128 // g_own)
    span = side * g_own
    nx = nf // 2
    order = [k for k in range(2, nf)] + [1, 0]
    arrive = [0, 1] + [k for k in range(2, nf)]

    def peer_of(k):
        return lax.rem(fi // 2 + k // 2, nx) * 2 + lax.rem(fi + k, 2)

    def source_of(k):
        return lax.rem(fi // 2 + nx - k // 2, nx) * 2 + lax.rem(fi + k, 2)

    def fetch_rows(k):
        j = peer_of(k)
        return pltpu.make_async_copy(
            design_hbm.at[pl.ds(pl.multiple_of(j * width, width), width), :],
            design.at[j],
            load_d.at[k],
        )

    def fetch(i):
        src, dst = (
            (beta_hbm, beta),
            (ids_hbm, ids),
            (pools_hbm, pools),
            (labels_hbm, labels),
            (pri_hbm, pri.at[li]),
            (step_hbm, step_s),
            (regions_hbm, regions),
            (pool_m_hbm, pool_m),
            (region_m_hbm, region_m),
            (beta_m_hbm, beta_m),
        )[i]
        return pltpu.make_async_copy(src, dst, load.at[i])

    for i in range(2):
        fetch(i).start()
    fetch_rows(order[0]).start()
    fetch(2).start()
    for k in order[1:]:
        fetch_rows(k).start()
    for i in range(3, 10):
        fetch(i).start()

    barrier = pltpu.get_barrier_semaphore()
    for k in range(1, nf):
        pl.semaphore_signal(
            barrier, inc=1, device_id={"feat": peer_of(k)}, device_id_type=MESH
        )
    for k in range(1, nl):
        pl.semaphore_signal(
            barrier, inc=1, device_id={"loan": lax.rem(li + k, nl)}, device_id_type=MESH
        )

    def remote(src, dst, ss, rs, axis, peer):
        return pltpu.make_async_remote_copy(
            src_ref=src,
            dst_ref=dst,
            send_sem=ss,
            recv_sem=rs,
            device_id={axis: peer},
            device_id_type=MESH,
        )

    def rs_copy(t, k):
        peer = peer_of(k)
        return remote(
            part.at[t, peer], rs_buf.at[t, k - 1], s_rs.at[t, k - 1], r_rs.at[t, k - 1], "feat", peer
        )

    def ag_copy(t, k, slot):
        return remote(
            resid.at[t, slot],
            resid.at[t, slot],
            s_ag.at[t, k - 1],
            r_ag.at[t, k - 1],
            "feat",
            peer_of(k),
        )

    def loan_peer(k):
        return lax.rem(li + k, nl)

    def loan_source(k):
        return lax.rem(li + nl - k, nl)

    def xt_copies(t, k):
        return [
            remote(
                ref.at[t, 0],
                ref.at[t, k],
                s_xt.at[i, t, k - 1],
                r_xt.at[i, t, k - 1],
                "loan",
                loan_peer(k),
            )
            for i, ref in enumerate((xt_s, xt_q))
        ]

    def rr_copies(t, k):
        peer = loan_peer(k)
        return [
            remote(
                src.at[t, peer],
                dst.at[t, k - 1],
                s_rr.at[i, t, k - 1],
                r_rr.at[i, t, k - 1],
                "loan",
                peer,
            )
            for i, (src, dst) in enumerate(((part_s, buf_s), (part_q, buf_q)))
        ]

    def ra_copies(t, k, owner):
        return [
            remote(
                ref.at[t, owner],
                ref.at[t, owner],
                s_ra.at[i, t, k - 1],
                r_ra.at[i, t, k - 1],
                "loan",
                loan_peer(k),
            )
            for i, ref in enumerate((all_s, all_q))
        ]

    def pr_copy(k, owner):
        return remote(
            pri.at[owner], pri.at[owner], s_pr.at[k - 1], r_pr.at[k - 1], "loan", loan_peer(k)
        )

    def onehot_t(row):
        return (row == lax.broadcasted_iota(jnp.int32, (n_reg, owned), 0)).astype(F32)

    def wide(ref, i):
        return jnp.concatenate([ref[i * side + c] for c in range(side)], axis=1)

    def cols(i):
        return pl.ds(i * span, span)

    n_cols = lanes // span

    def prologue():
        fetch(0).wait()
        lhs[pl.ds(0, chains), :] = beta[...].astype(BF16)
        lhs[pl.ds(chains, g_own), :] = (
            (
                lax.broadcasted_iota(jnp.int32, (g_own, feats), 1)
                == stride * lax.broadcasted_iota(jnp.int32, (g_own, feats), 0)
            )
            .astype(F32)
            .astype(BF16)
        )
        size = eye.shape[0]
        eye[...] = (
            (
                lax.broadcasted_iota(jnp.int32, (size, size), 0)
                == lax.broadcasted_iota(jnp.int32, (size, size), 1)
            )
            .astype(F32)
            .astype(BF16)
        )
        fetch(1).wait()

    def put_u4(c, blocks):
        hi, lo = halves(jnp.concatenate(blocks, axis=1))
        u4[pl.ds(c * prow, prow), :] = hi
        u4[pl.ds((chains + c) * prow, prow), :] = lo

    def slopes_first():
        fetch(2).wait()
        for c in range(chains):
            put_u4(c, [pools[c, pl.ds(k * prow, prow), :] for k in range(nb)])

    def slopes_next():
        for c in range(chains):
            put_u4(
                c,
                [
                    pools_n[pl.ds(k * prow, prow), pl.ds(c * g_own, g_own)]
                    for k in range(nb)
                ],
            )

    def pool_term(j):
        z = dot(u4[...], fold[j])
        m = mask[j]
        low = chains * prow
        for c in range(chains):
            a = z[c * prow : (c + 1) * prow] + z[low + c * prow : low + (c + 1) * prow]
            term[j, pl.ds(c, 1), :] = jnp.sum(a * m, axis=0, keepdims=True)

    first = li * owned

    def logits_first(k):
        j = peer_of(k)
        fetch_rows(k).wait()
        both = dot(lhs[...], design[j], NT)
        local = ids[j] - first
        block = local // prow
        mask[j] = (
            local - block * prow == lax.broadcasted_iota(jnp.int32, (prow, width), 0)
        ).astype(F32)
        slope = both[chains:]
        for b in range(nb):
            fold[j, pl.ds(b * g_own, g_own), :] = jnp.where(block == b, slope, 0.0).astype(BF16)
        pool_term(j)
        part[0, j] = term[j] + both[:chains]
        if k:
            rs_copy(0, k).start()

    def terms_next():
        for j in range(nf):
            pool_term(j)

    def flip(k):
        j = peer_of(k)
        size = eye.shape[0]
        for i in range(feats // size):
            x = dot(eye[...], design[j, :, pl.ds(i * size, size)], NT)
            flipped[j, pl.ds(i * size, size), :] = x.astype(BF16)

    def logits_next():
        b16 = beta_n[...].astype(BF16)
        for k in order:
            j = peer_of(k)
            part[1, j] = term[j] + dot(b16, flipped[j])
            if k:
                rs_copy(1, k).start()

    def residuals(t):
        logit = part[t, fi]
        for k in range(1, nf):
            rs_copy(t, k).wait_recv()
            logit = logit + rs_buf[t, k - 1]
        mine = (labels[fi].astype(F32) - jax.nn.sigmoid(logit)).astype(BF16)
        resid[t, fi] = mine
        for k in order[:-1]:
            ag_copy(t, k, fi).start()

    def population(t, k):
        s = source_of(k)
        if k:
            ag_copy(t, k, s).wait_recv()
        x = dot(resid[t, s], design[s])
        if k == arrive[0]:
            xt_f[...] = x
        elif k != arrive[-1]:
            xt_f[...] += x
        else:
            xt_q[t, 0], xt_s[t, 0] = code(xt_f[...] + x)

    def population_send(t):
        for k in range(1, nl):
            for copy in xt_copies(t, k):
                copy.start()

    def population_sum(t):
        for k in range(1, nl):
            for copy in xt_copies(t, k):
                copy.wait_recv()
        total = decode(xt_q[t, li], xt_s[t, li])
        for j in range(1, nl):
            slot = lax.rem(li + nl - j, nl)
            total = total + decode(xt_q[t, slot], xt_s[t, slot])
        return total

    def likelihood(t, k):
        s = source_of(k)
        resid_f[...] = resid[t, s].astype(F32)
        m = mask[s]
        a = jnp.concatenate(
            [(resid_f[pl.ds(c, 1), :] * m).astype(BF16) for c in range(chains)], axis=0
        )
        x = dot(a, fold[s], NT)
        if k == arrive[0]:
            lik[...] = x
        else:
            lik[...] += x

    def lik_cols(i):
        return jnp.concatenate(
            [
                jnp.concatenate(
                    [
                        lik[
                            pl.ds((i * side + c) * prow, prow), pl.ds(k * g_own, g_own)
                        ]
                        for c in range(side)
                    ],
                    axis=1,
                )
                for k in range(nb)
            ],
            axis=0,
        )

    def step_cols(i):
        lane = lax.broadcasted_iota(jnp.int32, (1, span), 1) // g_own
        e = jnp.zeros((1, span), F32)
        for c in range(side):
            e = jnp.where(lane == c, step_s[i * side + c], e)
        return e

    def region_sum(t, get):
        oht = onehot_t(pri[li])
        oht2 = jnp.concatenate([oht, oht], axis=1).astype(BF16)
        rows = n_reg // nl
        for i in range(n_cols):
            hi, lo = halves(get(i))
            s = dot(oht2, jnp.concatenate([hi, lo], axis=0))
            for o in range(nl):
                q, scale = code(s[o * rows : (o + 1) * rows])
                part_q[t, o, :, cols(i)] = q
                part_s[t, o, :, cols(i)] = scale

    def region_send(t):
        for k in range(1, nl):
            for copy in rr_copies(t, k):
                copy.start()

    def deviation(get_u, get_v):
        oht = onehot_t(pri[li])
        eye = (
            lax.broadcasted_iota(jnp.int32, (owned, owned), 0)
            == lax.broadcasted_iota(jnp.int32, (owned, owned), 1)
        ).astype(F32)
        oh = dot(eye.astype(BF16), oht.astype(BF16), NT)
        oh2 = jnp.concatenate([oh, oh], axis=1).astype(BF16)
        for i in range(n_cols):
            hi, lo = halves(get_v(i))
            dev[:, cols(i)] = PREC * (get_u(i) - dot(oh2, jnp.concatenate([hi, lo], axis=0)))

    def region_first():
        fetch(4).wait()
        region_sum(0, lambda i: wide(pools, i))
        for k in range(1, nl):
            pr_copy(k, li).start()
        region_send(0)

    def deviation_first():
        fetch(6).wait()
        deviation(lambda i: wide(pools, i), lambda i: wide(regions, i))

    def region_reduce(t):
        total = decode(part_q[t, li], part_s[t, li])
        for k in range(1, nl):
            for copy in rr_copies(t, k):
                copy.wait_recv()
            total = total + decode(buf_q[t, k - 1], buf_s[t, k - 1])
        all_q[t, li], all_s[t, li] = code(total)
        for k in range(1, nl):
            for copy in ra_copies(t, k, li):
                copy.start()

    def region_gather(t):
        for k in range(1, nl):
            for copy in ra_copies(t, k, loan_source(k)):
                copy.wait_recv()

    def counts():
        n = jnp.zeros((n_reg, 1), F32)
        for i in range(nl):
            n = n + jnp.sum(onehot_t(pri[i]), axis=1, keepdims=True)
        return n + 1.0

    def region_force(t, i, get_v, n):
        s = jnp.concatenate(
            [decode(all_q[t, o, :, cols(i)], all_s[t, o, :, cols(i)]) for o in range(nl)], axis=0
        )
        return PREC * (s - n * get_v(i))

    def wait_rest():
        fetch(3).wait()
        fetch(5).wait()

    def pool_update():
        fetch(7).wait()
        for i in range(n_cols):
            e = step_cols(i)
            m = wide(pool_m, i) + (0.5 * e) * (lik_cols(i) - dev[:, cols(i)])
            pool_mn[:, cols(i)] = m
            pools_n[:, cols(i)] = wide(pools, i) + e * m

    def region_next():
        fetch(8).wait()
        region_gather(0)
        for k in range(1, nl):
            pr_copy(k, loan_source(k)).wait_recv()
        n = counts()
        for i in range(n_cols):
            e = step_cols(i)
            g = region_force(0, i, lambda i: wide(regions, i), n)
            m = wide(region_m, i) + (0.5 * e) * g
            region_mn[:, cols(i)] = m
            regions_n[:, cols(i)] = wide(regions, i) + e * m
        deviation(lambda i: pools_n[:, cols(i)], lambda i: regions_n[:, cols(i)])

    def region_last():
        region_gather(1)
        n = counts()
        for i in range(n_cols):
            g = region_force(1, i, lambda i: regions_n[:, cols(i)], n)
            region_mn[:, cols(i)] += (0.5 * step_cols(i)) * g

    def pool_last():
        for i in range(n_cols):
            pool_mn[:, cols(i)] += (0.5 * step_cols(i)) * (lik_cols(i) - dev[:, cols(i)])

    def step_rows():
        chain = lax.broadcasted_iota(jnp.int32, (chains, 1), 0)
        e = jnp.zeros((chains, 1), F32)
        for c in range(chains):
            e = jnp.where(chain == c, step_s[c], e)
        return e

    def beta_next():
        fetch(9).wait()
        e = step_rows()
        m = beta_m[...] + (0.5 * e) * (population_sum(0) - total_feats * beta[...])
        beta_mn[...] = m
        beta_n[...] = beta[...] + e * m

    def beta_last():
        beta_mn[...] += (0.5 * step_rows()) * (population_sum(1) - total_feats * beta_n[...])

    def barrier_wait():
        pl.semaphore_wait(barrier, nf + nl - 2)

    def sum_next():
        region_sum(1, lambda i: pools_n[:, cols(i)])
        region_send(1)

    def sent():
        for t in range(2):
            for k in range(1, nf):
                rs_copy(t, k).wait_send()
                ag_copy(t, k, fi).wait_send()
            for k in range(1, nl):
                for copy in xt_copies(t, k) + rr_copies(t, k) + ra_copies(t, k, li):
                    copy.wait_send()
        for k in range(1, nl):
            pr_copy(k, li).wait_send()

    prologue()
    slopes_first()
    barrier_wait()
    for k in order:
        logits_first(k)
    region_first()
    deviation_first()
    wait_rest()
    residuals(0)
    for k in arrive[:2]:
        population(0, k)
        likelihood(0, k)
    flip(arrive[0])
    for k in arrive[2:]:
        population(0, k)
    population_send(0)
    for k in arrive[2:]:
        likelihood(0, k)
    pool_update()
    slopes_next()
    terms_next()
    sum_next()
    for k in arrive[1:]:
        flip(k)
    region_reduce(0)
    beta_next()
    logits_next()
    residuals(1)
    for k in arrive[:2]:
        population(1, k)
        likelihood(1, k)
    region_next()
    region_reduce(1)
    for k in arrive[2:]:
        population(1, k)
    population_send(1)
    for k in arrive[2:]:
        likelihood(1, k)
    pool_last()
    region_last()
    beta_last()
    sent()


def emit(
    beta_n,
    pools_n,
    regions_n,
    beta_mn,
    pool_mn,
    region_mn,
    beta_o,
    pools_o,
    regions_o,
    beta_mo,
    pool_mo,
    region_mo,
    pools_v,
    regions_v,
    pool_mv,
    region_mv,
    sem,
):
    pending = [
        pltpu.make_async_copy(beta_n, beta_o, sem.at[0]),
        pltpu.make_async_copy(beta_mn, beta_mo, sem.at[1]),
    ]
    for copy in pending:
        copy.start()
    wide = (
        (pools_n, pools_v, pools_o),
        (regions_n, regions_v, regions_o),
        (pool_mn, pool_mv, pool_mo),
        (region_mn, region_mv, region_mo),
    )
    for n, (src, tmp, dst) in enumerate(wide):
        chains, _, g_own = tmp.shape
        for c in range(chains):
            tmp[c] = src[:, pl.ds(c * g_own, g_own)]
        copy = pltpu.make_async_copy(tmp, dst, sem.at[2 + n])
        copy.start()
        pending.append(copy)
    for copy in pending:
        copy.wait()


def body(
    nf,
    nl,
    design,
    labels,
    pool_ids,
    pool_region_index,
    step_size,
    beta,
    pools,
    regions,
    beta_momentum,
    pool_momentum,
    region_momentum,
):
    loans, feats = design.shape
    chains, owned, g_own = pools.shape
    n_reg = regions.shape[1]
    width = loans // nf
    lanes = chains * g_own
    nb = blocks_of(owned, g_own)
    prow = owned // nb
    rows = n_reg // nl
    vmem = pl.BlockSpec(memory_space=pltpu.VMEM)
    hbm = pl.BlockSpec(memory_space=pltpu.HBM)
    dma = pltpu.SemaphoreType.DMA
    args = (
        design,
        labels.reshape(nf, 1, width),
        pool_ids.reshape(nf, 1, width),
        pool_region_index.reshape(1, owned),
        step_size,
        beta,
        pools,
        regions,
        beta_momentum,
        pool_momentum,
        region_momentum,
    )
    outs = (beta, pools, regions, beta_momentum, pool_momentum, region_momentum)
    packed = tuple(
        OUT(x.shape if x.ndim == 2 else (x.shape[1], lanes), F32) for x in outs
    )
    results = pl.pallas_call(
        functools.partial(kernel, nf, nl),
        out_shape=packed,
        in_specs=[hbm] * len(args),
        out_specs=tuple(vmem for _ in outs),
        scratch_shapes=[
            pltpu.VMEM((nf, width, feats), BF16),
            pltpu.VMEM((nf, 1, width), jnp.int32),
            pltpu.VMEM((nf, 1, width), jnp.int32),
            pltpu.VMEM((nl, 1, owned), jnp.int32),
            pltpu.SMEM(step_size.shape, F32),
            pltpu.VMEM(beta.shape, F32),
            pltpu.VMEM(pools.shape, F32),
            pltpu.VMEM(regions.shape, F32),
            pltpu.VMEM(beta.shape, F32),
            pltpu.VMEM(pools.shape, F32),
            pltpu.VMEM(regions.shape, F32),
            pltpu.VMEM((chains + g_own, feats), BF16),
            pltpu.VMEM((nf, prow, width), F32),
            pltpu.VMEM((nf, nb * g_own, width), BF16),
            pltpu.VMEM((2 * chains * prow, nb * g_own), BF16),
            pltpu.VMEM((chains * prow, nb * g_own), F32),
            pltpu.VMEM((nf, chains, width), F32),
            pltpu.VMEM((owned, lanes), F32),
            pltpu.VMEM((2, nf, chains, width), F32),
            pltpu.VMEM((2, nf - 1, chains, width), F32),
            pltpu.VMEM((2, nf, chains, width), BF16),
            pltpu.VMEM((chains, width), F32),
            pltpu.VMEM((chains, feats), F32),
            pltpu.VMEM((2, nl, chains, feats), I16),
            pltpu.VMEM((2, nl, 1, feats), F32),
            pltpu.VMEM((2, nl, rows, lanes), I16),
            pltpu.VMEM((2, nl, 1, lanes), F32),
            pltpu.VMEM((2, nl - 1, rows, lanes), I16),
            pltpu.VMEM((2, nl - 1, 1, lanes), F32),
            pltpu.VMEM((2, nl, rows, lanes), I16),
            pltpu.VMEM((2, nl, 1, lanes), F32),
            pltpu.VMEM((nf, feats, width), BF16),
            pltpu.VMEM((min(256, feats),) * 2, BF16),
            dma((10,)),
            dma((nf,)),
            dma((2, nf - 1)),
            dma((2, nf - 1)),
            dma((2, nf - 1)),
            dma((2, nf - 1)),
            dma((2, 2, nl - 1)),
            dma((2, 2, nl - 1)),
            dma((2, 2, nl - 1)),
            dma((2, 2, nl - 1)),
            dma((2, 2, nl - 1)),
            dma((2, 2, nl - 1)),
            dma((nl - 1,)),
            dma((nl - 1,)),
        ],
        compiler_params=pltpu.CompilerParams(
            collective_id=0, has_side_effects=True, vmem_limit_bytes=VLIM << 20
        ),
    )(*[pltpu.with_memory_space_constraint(x, pltpu.HBM) for x in args])
    return pl.pallas_call(
        emit,
        out_shape=tuple(jax.ShapeDtypeStruct(x.shape, x.dtype) for x in outs),
        in_specs=[vmem] * len(outs),
        out_specs=tuple(hbm for _ in outs),
        scratch_shapes=[
            pltpu.VMEM(pools.shape, F32),
            pltpu.VMEM(regions.shape, F32),
            pltpu.VMEM(pools.shape, F32),
            pltpu.VMEM(regions.shape, F32),
            dma((6,)),
        ],
        compiler_params=pltpu.CompilerParams(vmem_limit_bytes=16 << 20),
    )(*results)


VLIM = 24
OUT = pltpu.VMEM


def solution(mesh):
    in_specs = (
        P(("grp", "loan"), "feat"),
        P(("grp", "loan")),
        P(("grp", "loan")),
        P(("grp", "loan")),
        P("grp"),
        P("grp", "feat"),
        P("grp", "loan", "feat"),
        P("grp", None, "feat"),
        P("grp", "feat"),
        P("grp", "loan", "feat"),
        P("grp", None, "feat"),
    )
    out_specs = (
        P("grp", "feat"),
        P("grp", "loan", "feat"),
        P("grp", None, "feat"),
        P("grp", "feat"),
        P("grp", "loan", "feat"),
        P("grp", None, "feat"),
    )
    step = functools.partial(body, mesh.shape["feat"], mesh.shape["loan"])
    return jax.shard_map(step, mesh=mesh, in_specs=in_specs, out_specs=out_specs, check_vma=False)
```

```python
import functools

import jax
import jax.numpy as jnp
from jax import lax
from jax.experimental import pallas as pl
from jax.experimental.pallas import tpu as pltpu
from jax.sharding import PartitionSpec as P

PREC = 256.0
MESH = pl.DeviceIdType.MESH
NT = (((1,), (1,)), ((), ()))
NN = (((1,), (0,)), ((), ()))
F32 = jnp.float32
BF16 = jnp.bfloat16
I16 = jnp.int16
TOP = 32767.0


def dot(a, b, dims=NN):
    return lax.dot_general(a, b, dims, preferred_element_type=F32)


def halves(x):
    hi = x.astype(BF16)
    return hi, (x - hi.astype(F32)).astype(BF16)


def code(x):
    unit = min(128, x.shape[1])
    pieces = [x[:, i : i + unit] for i in range(0, x.shape[1], unit)]
    top = functools.reduce(jnp.maximum, [jnp.abs(p) for p in pieces])
    top = jnp.maximum(jnp.max(top, axis=0, keepdims=True), 1e-30)
    up = TOP / top
    q = jnp.concatenate([jnp.round(p * up).astype(jnp.int32).astype(I16) for p in pieces], axis=1)
    return q, top * (1.0 / TOP)


def decode(q, scale):
    unit = scale.shape[1]
    return jnp.concatenate(
        [
            q[:, i : i + unit].astype(jnp.int32).astype(F32) * scale
            for i in range(0, q.shape[1], unit)
        ],
        axis=1,
    )


def blocks_of(owned, g_own):
    return max(1, min(256 // g_own, owned // 16))


def kernel(
    nf,
    nl,
    design_hbm,
    labels_hbm,
    ids_hbm,
    pri_hbm,
    step_hbm,
    beta_hbm,
    pools_hbm,
    regions_hbm,
    beta_m_hbm,
    pool_m_hbm,
    region_m_hbm,
    beta_n,
    pools_n,
    regions_n,
    beta_mn,
    pool_mn,
    region_mn,
    pools_1,
    regions_1,
    pool_m1,
    region_m1,
    sums,
    design,
    labels,
    ids,
    pri,
    step_s,
    beta,
    pools,
    regions,
    beta_m,
    pool_m,
    region_m,
    lhs,
    mask,
    fold,
    u4,
    lik,
    term,
    dev,
    part,
    rs_buf,
    resid,
    resid_f,
    xt_f,
    xt_q,
    xt_s,
    part_q,
    part_s,
    buf_q,
    buf_s,
    all_q,
    all_s,
    flipped,
    eye,
    load,
    load_d,
    s_rs,
    r_rs,
    s_ag,
    r_ag,
    s_xt,
    r_xt,
    s_rr,
    r_rr,
    s_ra,
    r_ra,
    s_pr,
    r_pr,
):
    fi = lax.axis_index("feat")
    li = lax.axis_index("loan")
    chains, owned, g_own = pools.shape
    feats = beta.shape[1]
    n_reg = regions.shape[1]
    width = labels.shape[2]
    stride = feats // g_own
    total_feats = float(feats * nf)
    nb = blocks_of(owned, g_own)
    prow = owned // nb
    lanes = chains * g_own
    side = max(1, 128 // g_own)
    span = side * g_own
    nx = nf // 2
    order = [k for k in range(2, nf)] + [1, 0]
    arrive = [0, 1] + [k for k in range(2, nf)]

    def peer_of(k):
        return lax.rem(fi // 2 + k // 2, nx) * 2 + lax.rem(fi + k, 2)

    def source_of(k):
        return lax.rem(fi // 2 + nx - k // 2, nx) * 2 + lax.rem(fi + k, 2)

    def fetch_rows(k):
        j = peer_of(k)
        return pltpu.make_async_copy(
            design_hbm.at[pl.ds(pl.multiple_of(j * width, width), width), :],
            design.at[j],
            load_d.at[k],
        )

    def fetch(i):
        src, dst = (
            (beta_hbm, beta),
            (ids_hbm, ids),
            (pools_hbm, pools),
            (labels_hbm, labels),
            (pri_hbm, pri.at[li]),
            (step_hbm, step_s),
            (regions_hbm, regions),
            (pool_m_hbm, pool_m),
            (region_m_hbm, region_m),
            (beta_m_hbm, beta_m),
        )[i]
        return pltpu.make_async_copy(src, dst, load.at[i])

    for i in range(2):
        fetch(i).start()
    fetch_rows(order[0]).start()
    fetch(2).start()
    for k in order[1:]:
        fetch_rows(k).start()
    for i in range(3, 10):
        fetch(i).start()

    barrier = pltpu.get_barrier_semaphore()
    for k in range(1, nf):
        pl.semaphore_signal(
            barrier, inc=1, device_id={"feat": peer_of(k)}, device_id_type=MESH
        )
    for k in range(1, nl):
        pl.semaphore_signal(
            barrier, inc=1, device_id={"loan": lax.rem(li + k, nl)}, device_id_type=MESH
        )

    def remote(src, dst, ss, rs, axis, peer):
        return pltpu.make_async_remote_copy(
            src_ref=src,
            dst_ref=dst,
            send_sem=ss,
            recv_sem=rs,
            device_id={axis: peer},
            device_id_type=MESH,
        )

    def rs_copy(t, k):
        peer = peer_of(k)
        return remote(
            part.at[t, peer], rs_buf.at[t, k - 1], s_rs.at[t, k - 1], r_rs.at[t, k - 1], "feat", peer
        )

    def ag_copy(t, k, slot):
        return remote(
            resid.at[t, slot],
            resid.at[t, slot],
            s_ag.at[t, k - 1],
            r_ag.at[t, k - 1],
            "feat",
            peer_of(k),
        )

    def loan_peer(k):
        return lax.rem(li + k, nl)

    def loan_source(k):
        return lax.rem(li + nl - k, nl)

    def xt_copies(t, k):
        return [
            remote(
                ref.at[t, 0],
                ref.at[t, k],
                s_xt.at[i, t, k - 1],
                r_xt.at[i, t, k - 1],
                "loan",
                loan_peer(k),
            )
            for i, ref in enumerate((xt_s, xt_q))
        ]

    def rr_copies(t, k):
        peer = loan_peer(k)
        return [
            remote(
                src.at[t, peer],
                dst.at[t, k - 1],
                s_rr.at[i, t, k - 1],
                r_rr.at[i, t, k - 1],
                "loan",
                peer,
            )
            for i, (src, dst) in enumerate(((part_s, buf_s), (part_q, buf_q)))
        ]

    def ra_copies(t, k, owner):
        return [
            remote(
                ref.at[t, owner],
                ref.at[t, owner],
                s_ra.at[i, t, k - 1],
                r_ra.at[i, t, k - 1],
                "loan",
                loan_peer(k),
            )
            for i, ref in enumerate((all_s, all_q))
        ]

    def pr_copy(k, owner):
        return remote(
            pri.at[owner], pri.at[owner], s_pr.at[k - 1], r_pr.at[k - 1], "loan", loan_peer(k)
        )

    def onehot_t(row):
        return (row == lax.broadcasted_iota(jnp.int32, (n_reg, owned), 0)).astype(F32)

    def wide(ref, i):
        return jnp.concatenate([ref[i * side + c] for c in range(side)], axis=1)

    def cols(i):
        return pl.ds(i * span, span)

    n_cols = lanes // span

    def prologue():
        lhs[pl.ds(chains, g_own), :] = (
            (
                lax.broadcasted_iota(jnp.int32, (g_own, feats), 1)
                == stride * lax.broadcasted_iota(jnp.int32, (g_own, feats), 0)
            )
            .astype(F32)
            .astype(BF16)
        )
        size = eye.shape[0]
        eye[...] = (
            (
                lax.broadcasted_iota(jnp.int32, (size, size), 0)
                == lax.broadcasted_iota(jnp.int32, (size, size), 1)
            )
            .astype(F32)
            .astype(BF16)
        )

    def start_rows():
        fetch(0).wait()
        lhs[pl.ds(0, chains), :] = beta[...].astype(BF16)
        fetch(1).wait()

    def put_u4(c, blocks):
        hi, lo = halves(jnp.concatenate(blocks, axis=1))
        u4[pl.ds(c * prow, prow), :] = hi
        u4[pl.ds((chains + c) * prow, prow), :] = lo

    def slopes_first():
        fetch(2).wait()
        for c in range(chains):
            put_u4(c, [pools[c, pl.ds(k * prow, prow), :] for k in range(nb)])

    def slopes_next():
        for c in range(chains):
            put_u4(
                c,
                [
                    pools_1[pl.ds(k * prow, prow), pl.ds(c * g_own, g_own)]
                    for k in range(nb)
                ],
            )

    def pool_term(j):
        z = dot(u4[...], fold[j])
        m = mask[j]
        low = chains * prow
        for c in range(chains):
            a = z[c * prow : (c + 1) * prow] + z[low + c * prow : low + (c + 1) * prow]
            term[j, pl.ds(c, 1), :] = jnp.sum(a * m, axis=0, keepdims=True)

    first = li * owned

    def sweep(k):
        fetch_rows(k).wait()
        return dot(lhs[...], design[peer_of(k)], NT)

    def logits_first():
        both = sweep(order[0])
        for i, k in enumerate(order):
            ahead = sweep(order[i + 1]) if i + 1 < nf else None
            j = peer_of(k)
            local = ids[j] - first
            block = local // prow
            mask[j] = (
                local - block * prow == lax.broadcasted_iota(jnp.int32, (prow, width), 0)
            ).astype(F32)
            slope = both[chains:]
            for b in range(nb):
                fold[j, pl.ds(b * g_own, g_own), :] = jnp.where(block == b, slope, 0.0).astype(BF16)
            pool_term(j)
            part[0, j] = term[j] + both[:chains]
            if k:
                rs_copy(0, k).start()
            both = ahead

    def terms_next():
        for j in range(nf):
            pool_term(j)

    def flip(k):
        j = peer_of(k)
        size = eye.shape[0]
        for i in range(feats // size):
            x = dot(eye[...], design[j, :, pl.ds(i * size, size)], NT)
            flipped[j, pl.ds(i * size, size), :] = x.astype(BF16)

    def logits_next():
        b16 = beta_n[...].astype(BF16)
        for k in order:
            j = peer_of(k)
            part[1, j] = term[j] + dot(b16, flipped[j])
            if k:
                rs_copy(1, k).start()

    def residuals(t):
        logit = part[t, fi]
        for k in range(1, nf):
            rs_copy(t, k).wait_recv()
            logit = logit + rs_buf[t, k - 1]
        mine = (labels[fi].astype(F32) - jax.nn.sigmoid(logit)).astype(BF16)
        resid[t, fi] = mine
        for k in order[:-1]:
            ag_copy(t, k, fi).start()

    def population(t, k):
        s = source_of(k)
        if k:
            ag_copy(t, k, s).wait_recv()
        x = dot(resid[t, s], design[s])
        if k == arrive[0]:
            xt_f[...] = x
        elif k != arrive[-1]:
            xt_f[...] += x
        else:
            xt_q[t, 0], xt_s[t, 0] = code(xt_f[...] + x)

    def population_send(t):
        for k in range(1, nl):
            for copy in xt_copies(t, k):
                copy.start()

    def population_sum(t):
        for k in range(1, nl):
            for copy in xt_copies(t, k):
                copy.wait_recv()
        total = decode(xt_q[t, li], xt_s[t, li])
        for j in range(1, nl):
            slot = lax.rem(li + nl - j, nl)
            total = total + decode(xt_q[t, slot], xt_s[t, slot])
        return total

    def likelihood(t, k):
        s = source_of(k)
        resid_f[...] = resid[t, s].astype(F32)
        m = mask[s]
        a = jnp.concatenate(
            [(resid_f[pl.ds(c, 1), :] * m).astype(BF16) for c in range(chains)], axis=0
        )
        x = dot(a, fold[s], NT)
        if k == arrive[0]:
            lik[...] = x
        else:
            lik[...] += x

    def lik_cols(i):
        return jnp.concatenate(
            [
                jnp.concatenate(
                    [
                        lik[
                            pl.ds((i * side + c) * prow, prow), pl.ds(k * g_own, g_own)
                        ]
                        for c in range(side)
                    ],
                    axis=1,
                )
                for k in range(nb)
            ],
            axis=0,
        )

    def step_cols(i):
        lane = lax.broadcasted_iota(jnp.int32, (1, span), 1) // g_own
        e = jnp.zeros((1, span), F32)
        for c in range(side):
            e = jnp.where(lane == c, step_s[i * side + c], e)
        return e

    def region_sum(t, get):
        oht = onehot_t(pri[li])
        oht2 = jnp.concatenate([oht, oht], axis=1).astype(BF16)
        rows = n_reg // nl
        for i in range(n_cols):
            hi, lo = halves(get(i))
            sums[:, :, cols(i)] = dot(oht2, jnp.concatenate([hi, lo], axis=0)).reshape(
                nl, rows, span
            )
        for o in range(nl):
            part_q[t, o], part_s[t, o] = code(sums[o])

    def region_send(t):
        for k in range(1, nl):
            for copy in rr_copies(t, k):
                copy.start()

    def deviation(get_u, get_v):
        oht = onehot_t(pri[li])
        eye = (
            lax.broadcasted_iota(jnp.int32, (owned, owned), 0)
            == lax.broadcasted_iota(jnp.int32, (owned, owned), 1)
        ).astype(F32)
        oh = dot(eye.astype(BF16), oht.astype(BF16), NT)
        oh2 = jnp.concatenate([oh, oh], axis=1).astype(BF16)
        for i in range(n_cols):
            hi, lo = halves(get_v(i))
            dev[:, cols(i)] = PREC * (get_u(i) - dot(oh2, jnp.concatenate([hi, lo], axis=0)))

    def region_first():
        fetch(4).wait()
        region_sum(0, lambda i: wide(pools, i))
        for k in range(1, nl):
            pr_copy(k, li).start()
        region_send(0)

    def deviation_first():
        fetch(6).wait()
        deviation(lambda i: wide(pools, i), lambda i: wide(regions, i))

    def region_reduce(t):
        total = decode(part_q[t, li], part_s[t, li])
        for k in range(1, nl):
            for copy in rr_copies(t, k):
                copy.wait_recv()
            total = total + decode(buf_q[t, k - 1], buf_s[t, k - 1])
        all_q[t, li], all_s[t, li] = code(total)
        for k in range(1, nl):
            for copy in ra_copies(t, k, li):
                copy.start()

    def region_gather(t):
        for k in range(1, nl):
            for copy in ra_copies(t, k, loan_source(k)):
                copy.wait_recv()

    def counts():
        n = jnp.zeros((n_reg, 1), F32)
        for i in range(nl):
            n = n + jnp.sum(onehot_t(pri[i]), axis=1, keepdims=True)
        return n + 1.0

    def region_force(t, i, get_v, n):
        s = jnp.concatenate(
            [decode(all_q[t, o, :, cols(i)], all_s[t, o]) for o in range(nl)], axis=0
        )
        return PREC * (s - n * get_v(i))

    def wait_rest():
        fetch(3).wait()
        fetch(5).wait()

    def pool_update():
        fetch(7).wait()
        for i in range(n_cols):
            e = step_cols(i)
            m = wide(pool_m, i) + (0.5 * e) * (lik_cols(i) - dev[:, cols(i)])
            pool_m1[:, cols(i)] = m
            pools_1[:, cols(i)] = wide(pools, i) + e * m

    def region_next():
        fetch(8).wait()
        region_gather(0)
        for k in range(1, nl):
            pr_copy(k, loan_source(k)).wait_recv()
        n = counts()
        for i in range(n_cols):
            e = step_cols(i)
            g = region_force(0, i, lambda i: wide(regions, i), n)
            m = wide(region_m, i) + (0.5 * e) * g
            region_m1[:, cols(i)] = m
            regions_1[:, cols(i)] = wide(regions, i) + e * m
        deviation(lambda i: pools_1[:, cols(i)], lambda i: regions_1[:, cols(i)])

    def region_last():
        region_gather(1)
        n = counts()
        for i in range(n_cols):
            g = region_force(1, i, lambda i: regions_1[:, cols(i)], n)
            region_m1[:, cols(i)] += (0.5 * step_cols(i)) * g

    def pool_last():
        for i in range(n_cols):
            pool_m1[:, cols(i)] += (0.5 * step_cols(i)) * (lik_cols(i) - dev[:, cols(i)])

    def step_rows():
        chain = lax.broadcasted_iota(jnp.int32, (chains, 1), 0)
        e = jnp.zeros((chains, 1), F32)
        for c in range(chains):
            e = jnp.where(chain == c, step_s[c], e)
        return e

    def beta_next():
        fetch(9).wait()
        e = step_rows()
        m = beta_m[...] + (0.5 * e) * (population_sum(0) - total_feats * beta[...])
        beta_mn[...] = m
        beta_n[...] = beta[...] + e * m

    def beta_last():
        beta_mn[...] += (0.5 * step_rows()) * (population_sum(1) - total_feats * beta_n[...])

    def barrier_wait():
        pl.semaphore_wait(barrier, nf + nl - 2)

    def sum_next():
        region_sum(1, lambda i: pools_1[:, cols(i)])
        region_send(1)

    def sent():
        for t in range(2):
            for k in range(1, nf):
                rs_copy(t, k).wait_send()
                ag_copy(t, k, fi).wait_send()
            for k in range(1, nl):
                for copy in xt_copies(t, k) + rr_copies(t, k) + ra_copies(t, k, li):
                    copy.wait_send()
        for k in range(1, nl):
            pr_copy(k, li).wait_send()

    def unpack(src, dst):
        for c in range(chains):
            dst[c] = src[:, pl.ds(c * g_own, g_own)]

    prologue()
    start_rows()
    slopes_first()
    barrier_wait()
    logits_first()
    region_first()
    deviation_first()
    wait_rest()
    residuals(0)
    for k in arrive[:2]:
        population(0, k)
        likelihood(0, k)
    flip(arrive[0])
    for k in arrive[2:]:
        population(0, k)
    population_send(0)
    for k in arrive[2:]:
        likelihood(0, k)
    pool_update()
    slopes_next()
    terms_next()
    sum_next()
    for k in arrive[1:]:
        flip(k)
    region_reduce(0)
    beta_next()
    logits_next()
    unpack(pools_1, pools_n)
    residuals(1)
    for k in arrive[:2]:
        population(1, k)
        likelihood(1, k)
    region_reduce(1)
    for k in arrive[2:]:
        population(1, k)
    population_send(1)
    for k in arrive[2:]:
        likelihood(1, k)
    region_next()
    unpack(regions_1, regions_n)
    pool_last()
    unpack(pool_m1, pool_mn)
    region_last()
    unpack(region_m1, region_mn)
    beta_last()
    sent()


def emit(*refs):
    n = len(refs) // 2
    copies = [
        pltpu.make_async_copy(refs[i], refs[n + i], refs[-1].at[i]) for i in range(n)
    ]
    for copy in copies:
        copy.start()
    for copy in copies:
        copy.wait()


def body(
    nf,
    nl,
    design,
    labels,
    pool_ids,
    pool_region_index,
    step_size,
    beta,
    pools,
    regions,
    beta_momentum,
    pool_momentum,
    region_momentum,
):
    loans, feats = design.shape
    chains, owned, g_own = pools.shape
    n_reg = regions.shape[1]
    width = loans // nf
    lanes = chains * g_own
    nb = blocks_of(owned, g_own)
    prow = owned // nb
    rows = n_reg // nl
    vmem = pl.BlockSpec(memory_space=pltpu.VMEM)
    hbm = pl.BlockSpec(memory_space=pltpu.HBM)
    dma = pltpu.SemaphoreType.DMA
    args = (
        design,
        labels.reshape(nf, 1, width),
        pool_ids.reshape(nf, 1, width),
        pool_region_index.reshape(1, owned),
        step_size,
        beta,
        pools,
        regions,
        beta_momentum,
        pool_momentum,
        region_momentum,
    )
    outs = (beta, pools, regions, beta_momentum, pool_momentum, region_momentum)
    results = pl.pallas_call(
        functools.partial(kernel, nf, nl),
        out_shape=tuple(pltpu.VMEM(x.shape, F32) for x in outs),
        in_specs=[hbm] * len(args),
        out_specs=tuple(vmem for _ in outs),
        scratch_shapes=[
            pltpu.VMEM((owned, lanes), F32),
            pltpu.VMEM((n_reg, lanes), F32),
            pltpu.VMEM((owned, lanes), F32),
            pltpu.VMEM((n_reg, lanes), F32),
            pltpu.VMEM((nl, rows, lanes), F32),
            pltpu.VMEM((nf, width, feats), BF16),
            pltpu.VMEM((nf, 1, width), jnp.int32),
            pltpu.VMEM((nf, 1, width), jnp.int32),
            pltpu.VMEM((nl, 1, owned), jnp.int32),
            pltpu.SMEM(step_size.shape, F32),
            pltpu.VMEM(beta.shape, F32),
            pltpu.VMEM(pools.shape, F32),
            pltpu.VMEM(regions.shape, F32),
            pltpu.VMEM(beta.shape, F32),
            pltpu.VMEM(pools.shape, F32),
            pltpu.VMEM(regions.shape, F32),
            pltpu.VMEM((chains + g_own, feats), BF16),
            pltpu.VMEM((nf, prow, width), F32),
            pltpu.VMEM((nf, nb * g_own, width), BF16),
            pltpu.VMEM((2 * chains * prow, nb * g_own), BF16),
            pltpu.VMEM((chains * prow, nb * g_own), F32),
            pltpu.VMEM((nf, chains, width), F32),
            pltpu.VMEM((owned, lanes), F32),
            pltpu.VMEM((2, nf, chains, width), F32),
            pltpu.VMEM((2, nf - 1, chains, width), F32),
            pltpu.VMEM((2, nf, chains, width), BF16),
            pltpu.VMEM((chains, width), F32),
            pltpu.VMEM((chains, feats), F32),
            pltpu.VMEM((2, nl, chains, feats), I16),
            pltpu.VMEM((2, nl, 1, min(128, feats)), F32),
            pltpu.VMEM((2, nl, rows, lanes), I16),
            pltpu.VMEM((2, nl, 1, min(128, lanes)), F32),
            pltpu.VMEM((2, nl - 1, rows, lanes), I16),
            pltpu.VMEM((2, nl - 1, 1, min(128, lanes)), F32),
            pltpu.VMEM((2, nl, rows, lanes), I16),
            pltpu.VMEM((2, nl, 1, min(128, lanes)), F32),
            pltpu.VMEM((nf, feats, width), BF16),
            pltpu.VMEM((min(256, feats),) * 2, BF16),
            dma((10,)),
            dma((nf,)),
            dma((2, nf - 1)),
            dma((2, nf - 1)),
            dma((2, nf - 1)),
            dma((2, nf - 1)),
            dma((2, 2, nl - 1)),
            dma((2, 2, nl - 1)),
            dma((2, 2, nl - 1)),
            dma((2, 2, nl - 1)),
            dma((2, 2, nl - 1)),
            dma((2, 2, nl - 1)),
            dma((nl - 1,)),
            dma((nl - 1,)),
        ],
        compiler_params=pltpu.CompilerParams(
            collective_id=0, has_side_effects=True, vmem_limit_bytes=VLIM << 20
        ),
    )(*[pltpu.with_memory_space_constraint(x, pltpu.HBM) for x in args])
    return pl.pallas_call(
        emit,
        out_shape=tuple(jax.ShapeDtypeStruct(x.shape, x.dtype) for x in outs),
        in_specs=[vmem] * len(outs),
        out_specs=tuple(hbm for _ in outs),
        scratch_shapes=[dma((len(outs),))],
        compiler_params=pltpu.CompilerParams(vmem_limit_bytes=16 << 20),
    )(*results)


VLIM = 30


def solution(mesh):
    in_specs = (
        P(("grp", "loan"), "feat"),
        P(("grp", "loan")),
        P(("grp", "loan")),
        P(("grp", "loan")),
        P("grp"),
        P("grp", "feat"),
        P("grp", "loan", "feat"),
        P("grp", None, "feat"),
        P("grp", "feat"),
        P("grp", "loan", "feat"),
        P("grp", None, "feat"),
    )
    out_specs = (
        P("grp", "feat"),
        P("grp", "loan", "feat"),
        P("grp", None, "feat"),
        P("grp", "feat"),
        P("grp", "loan", "feat"),
        P("grp", None, "feat"),
    )
    step = functools.partial(body, mesh.shape["feat"], mesh.shape["loan"])
    return jax.shard_map(step, mesh=mesh, in_specs=in_specs, out_specs=out_specs, check_vma=False)
```

```python
import functools

import jax
import jax.numpy as jnp
from jax import lax
from jax.experimental import pallas as pl
from jax.experimental.pallas import tpu as pltpu
from jax.sharding import PartitionSpec as P

PREC = 256.0
MESH = pl.DeviceIdType.MESH
NT = (((1,), (1,)), ((), ()))
NN = (((1,), (0,)), ((), ()))
F32 = jnp.float32
BF16 = jnp.bfloat16
I16 = jnp.int16
TOP = 32767.0


def dot(a, b, dims=NN):
    return lax.dot_general(a, b, dims, preferred_element_type=F32)


def halves(x):
    hi = x.astype(BF16)
    return hi, (x - hi.astype(F32)).astype(BF16)


def code(x):
    unit = min(128, x.shape[1])
    pieces = [x[:, i : i + unit] for i in range(0, x.shape[1], unit)]
    top = functools.reduce(jnp.maximum, [jnp.abs(p) for p in pieces])
    top = jnp.maximum(jnp.max(top, axis=0, keepdims=True), 1e-30)
    up = TOP / top
    q = jnp.concatenate([jnp.round(p * up).astype(jnp.int32).astype(I16) for p in pieces], axis=1)
    return q, top * (1.0 / TOP)


def code_cols(x):
    top = jnp.maximum(jnp.max(jnp.abs(x), axis=0, keepdims=True), 1e-30)
    return jnp.round(x * (TOP / top)).astype(jnp.int32).astype(I16), top * (1.0 / TOP)


def decode(q, scale):
    unit = scale.shape[1]
    return jnp.concatenate(
        [
            q[:, i : i + unit].astype(jnp.int32).astype(F32) * scale
            for i in range(0, q.shape[1], unit)
        ],
        axis=1,
    )


def blocks_of(owned, g_own):
    return max(1, min(256 // g_own, owned // 16))


def kernel(
    nf,
    nl,
    design_hbm,
    labels_hbm,
    ids_hbm,
    pri_hbm,
    step_hbm,
    beta_hbm,
    pools_hbm,
    regions_hbm,
    beta_m_hbm,
    pool_m_hbm,
    region_m_hbm,
    beta_n,
    pools_n,
    regions_n,
    beta_mn,
    pool_mn,
    region_mn,
    pools_1,
    regions_1,
    pool_m1,
    region_m1,
    sums,
    design,
    labels,
    ids,
    pri,
    step_s,
    beta,
    pools,
    regions,
    beta_m,
    pool_m,
    region_m,
    lhs,
    mask,
    fold,
    u4,
    lik,
    term,
    dev,
    part,
    line_q,
    line_s,
    resid_f,
    xt_f,
    xt_q,
    xt_s,
    part_q,
    part_s,
    buf_q,
    buf_s,
    all_q,
    all_s,
    flipped,
    eye,
    load,
    load_d,
    s_lx,
    r_lx,
    s_xt,
    r_xt,
    s_rr,
    r_rr,
    s_ra,
    r_ra,
    s_pr,
    r_pr,
):
    fi = lax.axis_index("feat")
    li = lax.axis_index("loan")
    chains, owned, g_own = pools.shape
    feats = beta.shape[1]
    n_reg = regions.shape[1]
    width = labels.shape[2]
    stride = feats // g_own
    total_feats = float(feats * nf)
    nb = blocks_of(owned, g_own)
    prow = owned // nb
    lanes = chains * g_own
    side = max(1, 128 // g_own)
    span = side * g_own
    nx = nf // 2

    def peer_of(k):
        return lax.rem(fi // 2 + k // 2, nx) * 2 + lax.rem(fi + k, 2)

    def each(n, act):
        if n <= 4:
            for k in range(n - 1, 0, -1):
                act(k)
        else:

            def step(k, carry):
                act(k)
                return carry

            lax.fori_loop(1, n, step, 0)

    def fetch_rows(j):
        return pltpu.make_async_copy(
            design_hbm.at[pl.ds(j * width, width), :],
            design.at[j],
            load_d.at[j],
        )

    def fetch(i):
        src, dst = (
            (beta_hbm, beta),
            (ids_hbm, ids),
            (pools_hbm, pools),
            (labels_hbm, labels),
            (pri_hbm, pri.at[li]),
            (step_hbm, step_s),
            (regions_hbm, regions),
            (pool_m_hbm, pool_m),
            (region_m_hbm, region_m),
            (beta_m_hbm, beta_m),
        )[i]
        return pltpu.make_async_copy(src, dst, load.at[i])

    barrier = pltpu.get_barrier_semaphore()
    for k in range(nl - 1, 0, -1):
        pl.semaphore_signal(
            barrier, inc=1, device_id={"loan": lax.rem(li + k, nl)}, device_id_type=MESH
        )
    each(
        nf,
        lambda k: pl.semaphore_signal(
            barrier, inc=1, device_id={"feat": peer_of(k)}, device_id_type=MESH
        ),
    )

    for i in range(2):
        fetch(i).start()
    fetch_rows(0).start()
    fetch(2).start()
    fetch_rows(1).start()

    def remote(src, dst, ss, rs, axis, peer):
        return pltpu.make_async_remote_copy(
            src_ref=src,
            dst_ref=dst,
            send_sem=ss,
            recv_sem=rs,
            device_id={axis: peer},
            device_id_type=MESH,
        )

    batch = (1, 2 - nf % 2)

    def line_copies(t, k, j):
        some = pl.ds(j, batch[t])
        return [
            remote(
                ref.at[t, 0, some],
                ref.at[t, k, some],
                s_lx.at[i],
                r_lx.at[i, t, j],
                "feat",
                peer_of(k),
            )
            for i, ref in enumerate((line_s, line_q))
        ]

    def line_send(t, j, x):
        part[t, j] = x
        line_q[t, 0, j], line_s[t, 0, j] = code_cols(x)
        if t == 0 and j == 0:
            pl.semaphore_wait(barrier, nf + nl - 2)

        last = j - batch[t] + 1

        def go(k):
            for copy in line_copies(t, k, last):
                copy.start()

        if last % batch[t] == 0:
            each(nf, go)

    def settle(view, sem):
        pltpu.make_async_copy(view, view, sem).wait()

    others_f, others_l = pl.ds(1, nf - 1), pl.ds(1, nl - 1)

    def loan_peer(k):
        return lax.rem(li + k, nl)

    def xt_copies(t, k):
        return [
            remote(
                ref.at[t, 0],
                ref.at[t, k],
                s_xt.at[i],
                r_xt.at[i, t],
                "loan",
                loan_peer(k),
            )
            for i, ref in enumerate((xt_s, xt_q))
        ]

    def rr_copies(t, k):
        peer = loan_peer(k)
        return [
            remote(
                src.at[t, peer],
                dst.at[t, k - 1],
                s_rr.at[i],
                r_rr.at[i, t],
                "loan",
                peer,
            )
            for i, (src, dst) in enumerate(((part_s, buf_s), (part_q, buf_q)))
        ]

    def ra_copies(t, k, owner):
        return [
            remote(
                ref.at[t, owner],
                ref.at[t, owner],
                s_ra.at[i],
                r_ra.at[i, t],
                "loan",
                loan_peer(k),
            )
            for i, ref in enumerate((all_s, all_q))
        ]

    def pr_copy(k, owner):
        return remote(
            pri.at[owner], pri.at[owner], s_pr, r_pr, "loan", loan_peer(k)
        )

    def onehot_t(row):
        return (row == lax.broadcasted_iota(jnp.int32, (n_reg, owned), 0)).astype(F32)

    def wide(ref, i):
        return jnp.concatenate([ref[i * side + c] for c in range(side)], axis=1)

    def cols(i):
        return pl.ds(i * span, span)

    n_cols = lanes // span

    def prologue():
        size = eye.shape[0]
        tile = size // stride
        pick = (
            (
                lax.broadcasted_iota(jnp.int32, (tile, size), 1)
                == stride * lax.broadcasted_iota(jnp.int32, (tile, size), 0)
            )
            .astype(F32)
            .astype(BF16)
        )
        for i in range(feats // size):
            lhs[pl.ds(chains, tile), pl.ds(i * size, size)] = pick
        eye[...] = (
            (
                lax.broadcasted_iota(jnp.int32, (size, size), 0)
                == lax.broadcasted_iota(jnp.int32, (size, size), 1)
            )
            .astype(F32)
            .astype(BF16)
        )

    def start_rows():
        fetch(0).wait()
        for j in range(2, nf):
            fetch_rows(j).start()
        lhs[pl.ds(0, chains), :] = beta[...].astype(BF16)
        fetch(1).wait()

    def put_u4(c, blocks):
        hi, lo = halves(jnp.concatenate(blocks, axis=1))
        u4[pl.ds(c * prow, prow), :] = hi
        u4[pl.ds((chains + c) * prow, prow), :] = lo

    def slopes_first():
        fetch(2).wait()
        for c in range(chains):
            put_u4(c, [pools[c, pl.ds(k * prow, prow), :] for k in range(nb)])

    def slopes_next():
        for c in range(chains):
            put_u4(
                c,
                [
                    pools_1[pl.ds(k * prow, prow), pl.ds(c * g_own, g_own)]
                    for k in range(nb)
                ],
            )

    def pool_term(j):
        z = dot(u4[...], fold[j])
        m = mask[j]
        low = chains * prow
        for c in range(chains):
            a = z[c * prow : (c + 1) * prow] + z[low + c * prow : low + (c + 1) * prow]
            term[j, pl.ds(c, 1), :] = jnp.sum(a * m, axis=0, keepdims=True)

    first = li * owned

    turned = 2

    def sweep(j):
        fetch_rows(j).wait()
        size = eye.shape[0]
        line, slope = None, []
        for i in range(feats // size):
            if i < turned:
                y = design[j, :, pl.ds(i * size, size)].T
                flipped[j, pl.ds(i * size, size), :] = y
                x = dot(lhs[:, pl.ds(i * size, size)], y)
            else:
                x = dot(lhs[:, pl.ds(i * size, size)], design[j, :, pl.ds(i * size, size)], NT)
            line = x[:chains] if line is None else line + x[:chains]
            slope.append(x[chains:])
        return line, jnp.concatenate(slope, axis=0)

    def logits_first():
        both = sweep(0)
        for j in range(nf):
            ahead = sweep(j + 1) if j + 1 < nf else None
            local = ids[j] - first
            block = local // prow
            mask[j] = (
                local - block * prow == lax.broadcasted_iota(jnp.int32, (prow, width), 0)
            ).astype(F32)
            line, slope = both
            for b in range(nb):
                fold[j, pl.ds(b * g_own, g_own), :] = jnp.where(block == b, slope, 0.0).astype(BF16)
            pool_term(j)
            line_send(0, j, term[j] + line)
            if j == 0:
                for i in range(3, 10):
                    fetch(i).start()
            both = ahead

    def terms_next():
        for j in range(nf):
            pool_term(j)

    def flip(j):
        size = eye.shape[0]
        for i in range(turned, feats // size):
            x = dot(eye[...], design[j, :, pl.ds(i * size, size)], NT)
            flipped[j, pl.ds(i * size, size), :] = x.astype(BF16)

    def logits_next():
        b16 = beta_n[...].astype(BF16)
        for j in range(nf):
            line_send(1, j, term[j] + dot(b16, flipped[j]))

    def residual(t, j):
        if j % batch[t] == 0:
            some = pl.ds(j, batch[t])
            settle(line_s.at[t, others_f, some], r_lx.at[0, t, j])
            settle(line_q.at[t, others_f, some], r_lx.at[1, t, j])

        def add(k, logit):
            return logit + line_q[t, k, j].astype(jnp.int32).astype(F32) * line_s[t, k, j]

        logit = part[t, j]
        if nf <= 4:
            for k in range(1, nf):
                logit = add(k, logit)
        else:
            logit = lax.fori_loop(1, nf, add, logit)
        mine = (labels[j].astype(F32) - jax.nn.sigmoid(logit)).astype(BF16)
        resid_f[j] = mine.astype(F32)
        return mine

    def residuals(t, j):
        x = dot(residual(t, j), design[j])
        if j == 0:
            xt_f[...] = x
        elif j != nf - 1:
            xt_f[...] += x
        else:
            xt_q[t, 0], xt_s[t, 0] = code(xt_f[...] + x)

    def residuals_all(t):
        mine = [residual(t, j) for j in range(nf)]
        x = dot(mine[0], design[0])
        for j in range(1, nf):
            x = x + dot(mine[j], design[j])
        xt_q[t, 0], xt_s[t, 0] = code(x)

    def population_send(t):
        for k in range(1, nl):
            for copy in xt_copies(t, k):
                copy.start()

    def population_sum(t):
        settle(xt_s.at[t, others_l], r_xt.at[0, t])
        settle(xt_q.at[t, others_l], r_xt.at[1, t])
        total = decode(xt_q[t, li], xt_s[t, li])
        for j in range(1, nl):
            slot = lax.rem(li + nl - j, nl)
            total = total + decode(xt_q[t, slot], xt_s[t, slot])
        return total

    def likelihood(j):
        m = mask[j]
        a = jnp.concatenate(
            [(resid_f[j, pl.ds(c, 1), :] * m).astype(BF16) for c in range(chains)], axis=0
        )
        x = dot(a, fold[j], NT)
        if j == 0:
            lik[...] = x
        else:
            lik[...] += x

    def lik_cols(i):
        return jnp.concatenate(
            [
                jnp.concatenate(
                    [
                        lik[
                            pl.ds((i * side + c) * prow, prow), pl.ds(k * g_own, g_own)
                        ]
                        for c in range(side)
                    ],
                    axis=1,
                )
                for k in range(nb)
            ],
            axis=0,
        )

    def step_cols(i):
        lane = lax.broadcasted_iota(jnp.int32, (1, span), 1) // g_own
        e = jnp.zeros((1, span), F32)
        for c in range(side):
            e = jnp.where(lane == c, step_s[i * side + c], e)
        return e

    def region_sum(t, get):
        oht = onehot_t(pri[li])
        oht2 = jnp.concatenate([oht, oht], axis=1).astype(BF16)
        rows = n_reg // nl
        for i in range(n_cols):
            hi, lo = halves(get(i))
            sums[:, :, cols(i)] = dot(oht2, jnp.concatenate([hi, lo], axis=0)).reshape(
                nl, rows, span
            )
        for o in range(nl):
            part_q[t, o], part_s[t, o] = code(sums[o])

    def region_send(t):
        for k in range(1, nl):
            for copy in rr_copies(t, k):
                copy.start()

    def deviation(get_u, get_v):
        oht = onehot_t(pri[li])
        eye = (
            lax.broadcasted_iota(jnp.int32, (owned, owned), 0)
            == lax.broadcasted_iota(jnp.int32, (owned, owned), 1)
        ).astype(F32)
        oh = dot(eye.astype(BF16), oht.astype(BF16), NT)
        oh2 = jnp.concatenate([oh, oh], axis=1).astype(BF16)
        for i in range(n_cols):
            hi, lo = halves(get_v(i))
            dev[:, cols(i)] = PREC * (get_u(i) - dot(oh2, jnp.concatenate([hi, lo], axis=0)))

    def region_first():
        fetch(4).wait()
        region_sum(0, lambda i: wide(pools, i))
        for k in range(1, nl):
            pr_copy(k, li).start()
        region_send(0)

    def deviation_first():
        fetch(6).wait()
        deviation(lambda i: wide(pools, i), lambda i: wide(regions, i))

    def region_reduce(t):
        settle(buf_s.at[t], r_rr.at[0, t])
        settle(buf_q.at[t], r_rr.at[1, t])
        total = decode(part_q[t, li], part_s[t, li])
        for k in range(1, nl):
            total = total + decode(buf_q[t, k - 1], buf_s[t, k - 1])
        all_q[t, li], all_s[t, li] = code(total)
        for k in range(1, nl):
            for copy in ra_copies(t, k, li):
                copy.start()

    def region_gather(t):
        settle(all_s.at[t, others_l], r_ra.at[0, t])
        settle(all_q.at[t, others_l], r_ra.at[1, t])

    def counts():
        n = jnp.zeros((n_reg, 1), F32)
        for i in range(nl):
            n = n + jnp.sum(onehot_t(pri[i]), axis=1, keepdims=True)
        return n + 1.0

    def region_force(t, i, get_v, n):
        s = jnp.concatenate(
            [decode(all_q[t, o, :, cols(i)], all_s[t, o]) for o in range(nl)], axis=0
        )
        return PREC * (s - n * get_v(i))

    def wait_rest():
        fetch(3).wait()
        fetch(5).wait()

    def pool_update():
        fetch(7).wait()
        for i in range(n_cols):
            e = step_cols(i)
            m = wide(pool_m, i) + (0.5 * e) * (lik_cols(i) - dev[:, cols(i)])
            pool_m1[:, cols(i)] = m
            pools_1[:, cols(i)] = wide(pools, i) + e * m

    def region_next():
        fetch(8).wait()
        region_gather(0)
        settle(pri.at[others_l], r_pr)
        n = counts()
        for i in range(n_cols):
            e = step_cols(i)
            g = region_force(0, i, lambda i: wide(regions, i), n)
            m = wide(region_m, i) + (0.5 * e) * g
            region_m1[:, cols(i)] = m
            regions_1[:, cols(i)] = wide(regions, i) + e * m
        deviation(lambda i: pools_1[:, cols(i)], lambda i: regions_1[:, cols(i)])

    def region_last():
        region_gather(1)
        n = counts()
        for i in range(n_cols):
            g = region_force(1, i, lambda i: regions_1[:, cols(i)], n)
            region_m1[:, cols(i)] += (0.5 * step_cols(i)) * g

    def pool_last():
        for i in range(n_cols):
            pool_m1[:, cols(i)] += (0.5 * step_cols(i)) * (lik_cols(i) - dev[:, cols(i)])

    def step_rows():
        chain = lax.broadcasted_iota(jnp.int32, (chains, 1), 0)
        e = jnp.zeros((chains, 1), F32)
        for c in range(chains):
            e = jnp.where(chain == c, step_s[c], e)
        return e

    def beta_next():
        fetch(9).wait()
        e = step_rows()
        m = beta_m[...] + (0.5 * e) * (population_sum(0) - total_feats * beta[...])
        beta_mn[...] = m
        beta_n[...] = beta[...] + e * m

    def beta_last():
        beta_mn[...] += (0.5 * step_rows()) * (population_sum(1) - total_feats * beta_n[...])

    def sum_next():
        region_sum(1, lambda i: pools_1[:, cols(i)])
        region_send(1)

    def sent():
        settle(line_s.at[:, others_f], s_lx.at[0])
        settle(line_q.at[:, others_f], s_lx.at[1])
        settle(xt_s.at[:, others_l], s_xt.at[0])
        settle(xt_q.at[:, others_l], s_xt.at[1])
        settle(buf_s, s_rr.at[0])
        settle(buf_q, s_rr.at[1])
        settle(all_s.at[:, others_l], s_ra.at[0])
        settle(all_q.at[:, others_l], s_ra.at[1])
        settle(pri.at[others_l], s_pr)

    def unpack(src, dst):
        for c in range(chains):
            dst[c] = src[:, pl.ds(c * g_own, g_own)]

    prologue()
    start_rows()
    slopes_first()
    logits_first()
    region_first()
    deviation_first()
    wait_rest()
    for j in range(nf - 1):
        residuals(0, j)
        likelihood(j)
    residuals(0, nf - 1)
    population_send(0)
    likelihood(nf - 1)
    pool_update()
    slopes_next()
    terms_next()
    sum_next()
    for j in range(nf):
        flip(j)
    beta_next()
    logits_next()
    region_reduce(0)
    unpack(pools_1, pools_n)
    region_reduce(1)
    residuals_all(1)
    population_send(1)
    for j in range(nf):
        likelihood(j)
    region_next()
    unpack(regions_1, regions_n)
    pool_last()
    unpack(pool_m1, pool_mn)
    region_last()
    unpack(region_m1, region_mn)
    beta_last()
    sent()


def emit(*refs):
    n = len(refs) // 2
    copies = [
        pltpu.make_async_copy(refs[i], refs[n + i], refs[-1].at[i]) for i in range(n)
    ]
    for copy in copies:
        copy.start()
    for copy in copies:
        copy.wait()


def body(
    nf,
    nl,
    design,
    labels,
    pool_ids,
    pool_region_index,
    step_size,
    beta,
    pools,
    regions,
    beta_momentum,
    pool_momentum,
    region_momentum,
):
    loans, feats = design.shape
    chains, owned, g_own = pools.shape
    n_reg = regions.shape[1]
    width = loans // nf
    lanes = chains * g_own
    nb = blocks_of(owned, g_own)
    prow = owned // nb
    rows = n_reg // nl
    vmem = pl.BlockSpec(memory_space=pltpu.VMEM)
    hbm = pl.BlockSpec(memory_space=pltpu.HBM)
    dma = pltpu.SemaphoreType.DMA
    args = (
        design,
        labels.reshape(nf, 1, width),
        pool_ids.reshape(nf, 1, width),
        pool_region_index.reshape(1, owned),
        step_size,
        beta,
        pools,
        regions,
        beta_momentum,
        pool_momentum,
        region_momentum,
    )
    outs = (beta, pools, regions, beta_momentum, pool_momentum, region_momentum)
    results = pl.pallas_call(
        functools.partial(kernel, nf, nl),
        out_shape=tuple(pltpu.VMEM(x.shape, F32) for x in outs),
        in_specs=[hbm] * len(args),
        out_specs=tuple(vmem for _ in outs),
        scratch_shapes=[
            pltpu.VMEM((owned, lanes), F32),
            pltpu.VMEM((n_reg, lanes), F32),
            pltpu.VMEM((owned, lanes), F32),
            pltpu.VMEM((n_reg, lanes), F32),
            pltpu.VMEM((nl, rows, lanes), F32),
            pltpu.VMEM((nf, width, feats), BF16),
            pltpu.VMEM((nf, 1, width), jnp.int32),
            pltpu.VMEM((nf, 1, width), jnp.int32),
            pltpu.VMEM((nl, 1, owned), jnp.int32),
            pltpu.SMEM(step_size.shape, F32),
            pltpu.VMEM(beta.shape, F32),
            pltpu.VMEM(pools.shape, F32),
            pltpu.VMEM(regions.shape, F32),
            pltpu.VMEM(beta.shape, F32),
            pltpu.VMEM(pools.shape, F32),
            pltpu.VMEM(regions.shape, F32),
            pltpu.VMEM((chains + g_own * min(256, feats) // feats, feats), BF16),
            pltpu.VMEM((nf, prow, width), F32),
            pltpu.VMEM((nf, nb * g_own, width), BF16),
            pltpu.VMEM((2 * chains * prow, nb * g_own), BF16),
            pltpu.VMEM((chains * prow, nb * g_own), F32),
            pltpu.VMEM((nf, chains, width), F32),
            pltpu.VMEM((owned, lanes), F32),
            pltpu.VMEM((2, nf, chains, width), F32),
            pltpu.VMEM((2, nf, nf, chains, width), I16),
            pltpu.VMEM((2, nf, nf, 1, width), F32),
            pltpu.VMEM((nf, chains, width), F32),
            pltpu.VMEM((chains, feats), F32),
            pltpu.VMEM((2, nl, chains, feats), I16),
            pltpu.VMEM((2, nl, 1, min(128, feats)), F32),
            pltpu.VMEM((2, nl, rows, lanes), I16),
            pltpu.VMEM((2, nl, 1, min(128, lanes)), F32),
            pltpu.VMEM((2, nl - 1, rows, lanes), I16),
            pltpu.VMEM((2, nl - 1, 1, min(128, lanes)), F32),
            pltpu.VMEM((2, nl, rows, lanes), I16),
            pltpu.VMEM((2, nl, 1, min(128, lanes)), F32),
            pltpu.VMEM((nf, feats, width), BF16),
            pltpu.VMEM((min(256, feats),) * 2, BF16),
            dma((10,)),
            dma((nf,)),
            dma((2,)),
            dma((2, 2, nf)),
            dma((2,)),
            dma((2, 2)),
            dma((2,)),
            dma((2, 2)),
            dma((2,)),
            dma((2, 2)),
            dma,
            dma,
        ],
        compiler_params=pltpu.CompilerParams(
            collective_id=0, has_side_effects=True, vmem_limit_bytes=VLIM << 20
        ),
    )(*[pltpu.with_memory_space_constraint(x, pltpu.HBM) for x in args])
    return pl.pallas_call(
        emit,
        out_shape=tuple(jax.ShapeDtypeStruct(x.shape, x.dtype) for x in outs),
        in_specs=[vmem] * len(outs),
        out_specs=tuple(hbm for _ in outs),
        scratch_shapes=[dma((len(outs),))],
        compiler_params=pltpu.CompilerParams(vmem_limit_bytes=16 << 20),
    )(*results)


VLIM = 30


def solution(mesh):
    in_specs = (
        P(("grp", "loan"), "feat"),
        P(("grp", "loan")),
        P(("grp", "loan")),
        P(("grp", "loan")),
        P("grp"),
        P("grp", "feat"),
        P("grp", "loan", "feat"),
        P("grp", None, "feat"),
        P("grp", "feat"),
        P("grp", "loan", "feat"),
        P("grp", None, "feat"),
    )
    out_specs = (
        P("grp", "feat"),
        P("grp", "loan", "feat"),
        P("grp", None, "feat"),
        P("grp", "feat"),
        P("grp", "loan", "feat"),
        P("grp", None, "feat"),
    )
    step = functools.partial(body, mesh.shape["feat"], mesh.shape["loan"])
    return jax.shard_map(step, mesh=mesh, in_specs=in_specs, out_specs=out_specs, check_vma=False)
```

```python
import functools

import jax
import jax.numpy as jnp
from jax import lax
from jax.experimental import pallas as pl
from jax.experimental.pallas import tpu as pltpu
from jax.sharding import PartitionSpec as P

PREC = 256.0
MESH = pl.DeviceIdType.MESH
NT = (((1,), (1,)), ((), ()))
NN = (((1,), (0,)), ((), ()))
F32 = jnp.float32
BF16 = jnp.bfloat16
I16 = jnp.int16
TOP = 32767.0


def dot(a, b, dims=NN):
    return lax.dot_general(a, b, dims, preferred_element_type=F32)


def halves(x):
    hi = x.astype(BF16)
    return hi, (x - hi.astype(F32)).astype(BF16)


def code(x):
    unit = min(128, x.shape[1])
    pieces = [x[:, i : i + unit] for i in range(0, x.shape[1], unit)]
    top = functools.reduce(jnp.maximum, [jnp.abs(p) for p in pieces])
    top = jnp.maximum(jnp.max(top, axis=0, keepdims=True), 1e-30)
    up = TOP / top
    q = jnp.concatenate([jnp.round(p * up).astype(jnp.int32).astype(I16) for p in pieces], axis=1)
    return q, top * (1.0 / TOP)


def code_cols(x):
    top = jnp.maximum(jnp.max(jnp.abs(x), axis=0, keepdims=True), 1e-30)
    return jnp.round(x * (TOP / top)).astype(jnp.int32).astype(I16), top * (1.0 / TOP)


def decode(q, scale):
    unit = scale.shape[1]
    return jnp.concatenate(
        [
            q[:, i : i + unit].astype(jnp.int32).astype(F32) * scale
            for i in range(0, q.shape[1], unit)
        ],
        axis=1,
    )


def blocks_of(owned, g_own):
    return max(1, min(256 // g_own, owned // 16))


def kernel(
    nf,
    nl,
    design_hbm,
    labels_hbm,
    ids_hbm,
    pri_hbm,
    step_hbm,
    beta_hbm,
    pools_hbm,
    regions_hbm,
    beta_m_hbm,
    pool_m_hbm,
    region_m_hbm,
    beta_n,
    pools_n,
    regions_n,
    beta_mn,
    pool_mn,
    region_mn,
    pools_1,
    regions_1,
    pool_m1,
    region_m1,
    sums,
    design,
    labels,
    ids,
    pri,
    step_s,
    beta,
    pools,
    regions,
    beta_m,
    pool_m,
    region_m,
    lhs,
    mask,
    fold,
    u4,
    lik,
    term,
    dev,
    part,
    line_q,
    line_s,
    resid_f,
    xt_f,
    xt_q,
    xt_s,
    part_q,
    part_s,
    buf_q,
    buf_s,
    all_q,
    all_s,
    flipped,
    eye,
    load,
    load_d,
    s_lx,
    r_lx,
    s_xt,
    r_xt,
    s_rr,
    r_rr,
    s_ra,
    r_ra,
    s_pr,
    r_pr,
):
    fi = lax.axis_index("feat")
    li = lax.axis_index("loan")
    chains, owned, g_own = pools.shape
    feats = beta.shape[1]
    n_reg = regions.shape[1]
    width = labels.shape[2]
    stride = feats // g_own
    total_feats = float(feats * nf)
    nb = blocks_of(owned, g_own)
    prow = owned // nb
    lanes = chains * g_own
    side = max(1, 128 // g_own)
    span = side * g_own
    nx = nf // 2

    def peer_of(k):
        return lax.rem(fi // 2 + k // 2, nx) * 2 + lax.rem(fi + k, 2)

    def each(n, act):
        if n <= 4:
            for k in range(n - 1, 0, -1):
                act(k)
        else:

            def step(k, carry):
                act(k)
                return carry

            lax.fori_loop(1, n, step, 0)

    def fetch_rows(j):
        return pltpu.make_async_copy(
            design_hbm.at[pl.ds(j * width, width), :],
            design.at[j],
            load_d.at[j],
        )

    def fetch(i):
        src, dst = (
            (beta_hbm, beta),
            (ids_hbm, ids),
            (pools_hbm, pools),
            (labels_hbm, labels),
            (pri_hbm, pri.at[li]),
            (step_hbm, step_s),
            (regions_hbm, regions),
            (pool_m_hbm, pool_m),
            (region_m_hbm, region_m),
            (beta_m_hbm, beta_m),
        )[i]
        return pltpu.make_async_copy(src, dst, load.at[i])

    barrier = pltpu.get_barrier_semaphore()
    for k in range(nl - 1, 0, -1):
        pl.semaphore_signal(
            barrier, inc=1, device_id={"loan": lax.rem(li + k, nl)}, device_id_type=MESH
        )
    each(
        nf,
        lambda k: pl.semaphore_signal(
            barrier, inc=1, device_id={"feat": peer_of(k)}, device_id_type=MESH
        ),
    )

    for i in range(2):
        fetch(i).start()
    fetch_rows(0).start()
    fetch(2).start()
    fetch_rows(1).start()

    def remote(src, dst, ss, rs, axis, peer):
        return pltpu.make_async_remote_copy(
            src_ref=src,
            dst_ref=dst,
            send_sem=ss,
            recv_sem=rs,
            device_id={axis: peer},
            device_id_type=MESH,
        )

    batch = (1, 2 - nf % 2)

    def line_copies(t, k, j):
        some = pl.ds(j, batch[t])
        return [
            remote(
                ref.at[t, 0, some],
                ref.at[t, k, some],
                s_lx.at[i],
                r_lx.at[i, t, j],
                "feat",
                peer_of(k),
            )
            for i, ref in enumerate((line_s, line_q))
        ]

    def line_send(t, j, x):
        part[t, j] = x
        line_q[t, 0, j], line_s[t, 0, j] = code_cols(x)
        if t == 0 and j == 0:
            pl.semaphore_wait(barrier, nf + nl - 2)

        last = j - batch[t] + 1

        def go(k):
            for copy in line_copies(t, k, last):
                copy.start()

        if last % batch[t] == 0:
            each(nf, go)

    def settle(view, sem):
        pltpu.make_async_copy(view, view, sem).wait()

    others_f, others_l = pl.ds(1, nf - 1), pl.ds(1, nl - 1)

    def loan_peer(i):
        right = li // ((nl + 1) // 2)
        place = li * (1 - right) + (nl - 1 - li) * right
        far = nl - 1 - i - (place + 1 + i) // nl
        return far * (1 - right) + (nl - 1 - far) * right

    def loan_slot(peer):
        return lax.rem(peer - li + nl, nl)

    def xt_copies(t, k):
        peer = loan_peer(k)
        return [
            remote(
                ref.at[t, 0],
                ref.at[t, loan_slot(peer)],
                s_xt.at[i],
                r_xt.at[i, t],
                "loan",
                peer,
            )
            for i, ref in enumerate((xt_s, xt_q))
        ]

    def rr_copies(t, k):
        peer = loan_peer(k)
        return [
            remote(
                src.at[t, peer],
                dst.at[t, loan_slot(peer) - 1],
                s_rr.at[i],
                r_rr.at[i, t],
                "loan",
                peer,
            )
            for i, (src, dst) in enumerate(((part_s, buf_s), (part_q, buf_q)))
        ]

    def ra_copies(t, k, owner):
        return [
            remote(
                ref.at[t, owner],
                ref.at[t, owner],
                s_ra.at[i],
                r_ra.at[i, t],
                "loan",
                loan_peer(k),
            )
            for i, ref in enumerate((all_s, all_q))
        ]

    def pr_copy(k, owner):
        return remote(
            pri.at[owner], pri.at[owner], s_pr, r_pr, "loan", loan_peer(k)
        )

    def onehot_t(row):
        return (row == lax.broadcasted_iota(jnp.int32, (n_reg, owned), 0)).astype(F32)

    def wide(ref, i):
        return jnp.concatenate([ref[i * side + c] for c in range(side)], axis=1)

    def cols(i):
        return pl.ds(i * span, span)

    n_cols = lanes // span

    def prologue():
        size = eye.shape[0]
        tile = size // stride
        pick = (
            (
                lax.broadcasted_iota(jnp.int32, (tile, size), 1)
                == stride * lax.broadcasted_iota(jnp.int32, (tile, size), 0)
            )
            .astype(F32)
            .astype(BF16)
        )
        for i in range(feats // size):
            lhs[pl.ds(chains, tile), pl.ds(i * size, size)] = pick
        eye[...] = (
            (
                lax.broadcasted_iota(jnp.int32, (size, size), 0)
                == lax.broadcasted_iota(jnp.int32, (size, size), 1)
            )
            .astype(F32)
            .astype(BF16)
        )

    def start_rows():
        fetch(0).wait()
        for j in range(2, nf):
            fetch_rows(j).start()
        lhs[pl.ds(0, chains), :] = beta[...].astype(BF16)
        fetch(1).wait()

    def put_u4(c, blocks):
        hi, lo = halves(jnp.concatenate(blocks, axis=1))
        u4[pl.ds(c * prow, prow), :] = hi
        u4[pl.ds((chains + c) * prow, prow), :] = lo

    def slopes_first():
        fetch(2).wait()
        for c in range(chains):
            put_u4(c, [pools[c, pl.ds(k * prow, prow), :] for k in range(nb)])

    def slopes_next():
        for c in range(chains):
            put_u4(
                c,
                [
                    pools_1[pl.ds(k * prow, prow), pl.ds(c * g_own, g_own)]
                    for k in range(nb)
                ],
            )

    def pool_term(j):
        z = dot(u4[...], fold[j])
        m = mask[j]
        low = chains * prow
        for c in range(chains):
            a = z[c * prow : (c + 1) * prow] + z[low + c * prow : low + (c + 1) * prow]
            term[j, pl.ds(c, 1), :] = jnp.sum(a * m, axis=0, keepdims=True)

    first = li * owned

    turned = 2

    def sweep(j):
        fetch_rows(j).wait()
        size = eye.shape[0]
        line, slope = None, []
        for i in range(feats // size):
            depth = pl.ds(i * size, size)
            if i % 2 == 1 and i // 2 < turned or i == 0 and turned > 2:
                flipped[j, depth, :] = design[j, :, depth].T
                x = dot(lhs[:, depth], flipped[j, depth, :])
            else:
                x = dot(lhs[:, depth], design[j, :, depth], NT)
            line = x[:chains] if line is None else line + x[:chains]
            slope.append(x[chains:])
        local = ids[j] - first
        block = local // prow
        mask[j] = (
            local - block * prow == lax.broadcasted_iota(jnp.int32, (prow, width), 0)
        ).astype(F32)
        slope = jnp.concatenate(slope, axis=0)
        for b in range(nb):
            fold[j, pl.ds(b * g_own, g_own), :] = jnp.where(block == b, slope, 0.0).astype(BF16)
        part[0, j] = line

    def logits_first():
        sweep(0)
        for j in range(nf):
            if j + 1 < nf:
                sweep(j + 1)
            pool_term(j)
            line_send(0, j, term[j] + part[0, j])
            if j == 0:
                for i in (3, 4, 5, 6, 7, 8, 9):
                    fetch(i).start()

    def terms_next():
        for j in range(nf):
            pool_term(j)

    def flip(j):
        size = eye.shape[0]
        for i in range(feats // size):
            if i % 2 == 1 and i // 2 < turned or i == 0 and turned > 2:
                continue
            x = dot(eye[...], design[j, :, pl.ds(i * size, size)], NT)
            flipped[j, pl.ds(i * size, size), :] = x.astype(BF16)

    def logits_next():
        b16 = beta_n[...].astype(BF16)
        for j in range(nf):
            line_send(1, j, term[j] + dot(b16, flipped[j]))

    def residual(t, j):
        if j % batch[t] == 0:
            some = pl.ds(j, batch[t])
            settle(line_s.at[t, others_f, some], r_lx.at[0, t, j])
            settle(line_q.at[t, others_f, some], r_lx.at[1, t, j])

        def add(k, logit):
            return logit + line_q[t, k, j].astype(jnp.int32).astype(F32) * line_s[t, k, j]

        logit = part[t, j]
        if nf <= 4:
            for k in range(1, nf):
                logit = add(k, logit)
        else:
            logit = lax.fori_loop(1, nf, add, logit)
        mine = (labels[j].astype(F32) - jax.nn.sigmoid(logit)).astype(BF16)
        resid_f[j] = mine.astype(F32)
        return mine

    def residuals(t, j):
        x = dot(residual(t, j), design[j])
        if j == 0:
            xt_f[...] = x
        elif j != nf - 1:
            xt_f[...] += x
        else:
            xt_q[t, 0], xt_s[t, 0] = code(xt_f[...] + x)

    def residuals_all(t):
        mine = [residual(t, j) for j in range(nf)]
        x = dot(mine[0], design[0])
        for j in range(1, nf):
            x = x + dot(mine[j], design[j])
        xt_q[t, 0], xt_s[t, 0] = code(x)

    def population_send(t):
        for k in range(nl - 1):
            for copy in xt_copies(t, k):
                copy.start()

    def population_sum(t):
        settle(xt_s.at[t, others_l], r_xt.at[0, t])
        settle(xt_q.at[t, others_l], r_xt.at[1, t])
        total = decode(xt_q[t, li], xt_s[t, li])
        for j in range(1, nl):
            slot = lax.rem(li + nl - j, nl)
            total = total + decode(xt_q[t, slot], xt_s[t, slot])
        return total

    def likelihood(j):
        m = mask[j]
        a = jnp.concatenate(
            [(resid_f[j, pl.ds(c, 1), :] * m).astype(BF16) for c in range(chains)], axis=0
        )
        x = dot(a, fold[j], NT)
        if j == 0:
            lik[...] = x
        else:
            lik[...] += x

    def lik_cols(i):
        return jnp.concatenate(
            [
                jnp.concatenate(
                    [
                        lik[
                            pl.ds((i * side + c) * prow, prow), pl.ds(k * g_own, g_own)
                        ]
                        for c in range(side)
                    ],
                    axis=1,
                )
                for k in range(nb)
            ],
            axis=0,
        )

    def step_cols(i):
        lane = lax.broadcasted_iota(jnp.int32, (1, span), 1) // g_own
        e = jnp.zeros((1, span), F32)
        for c in range(side):
            e = jnp.where(lane == c, step_s[i * side + c], e)
        return e

    def region_sum(t, get):
        oht = onehot_t(pri[li])
        oht2 = jnp.concatenate([oht, oht], axis=1).astype(BF16)
        rows = n_reg // nl
        for i in range(n_cols):
            hi, lo = halves(get(i))
            sums[:, :, cols(i)] = dot(oht2, jnp.concatenate([hi, lo], axis=0)).reshape(
                nl, rows, span
            )
        for o in range(nl):
            part_q[t, o], part_s[t, o] = code(sums[o])

    def region_send(t):
        for k in range(nl - 1):
            for copy in rr_copies(t, k):
                copy.start()

    def deviation(get_u, get_v):
        oht = onehot_t(pri[li])
        eye = (
            lax.broadcasted_iota(jnp.int32, (owned, owned), 0)
            == lax.broadcasted_iota(jnp.int32, (owned, owned), 1)
        ).astype(F32)
        oh = dot(eye.astype(BF16), oht.astype(BF16), NT)
        oh2 = jnp.concatenate([oh, oh], axis=1).astype(BF16)
        for i in range(n_cols):
            hi, lo = halves(get_v(i))
            dev[:, cols(i)] = PREC * (get_u(i) - dot(oh2, jnp.concatenate([hi, lo], axis=0)))

    def region_first():
        fetch(4).wait()
        region_sum(0, lambda i: wide(pools, i))
        for k in range(nl - 1):
            pr_copy(k, li).start()
        region_send(0)

    def deviation_first():
        fetch(6).wait()
        deviation(lambda i: wide(pools, i), lambda i: wide(regions, i))

    def region_reduce(t):
        settle(buf_s.at[t], r_rr.at[0, t])
        settle(buf_q.at[t], r_rr.at[1, t])
        total = decode(part_q[t, li], part_s[t, li])
        for k in range(1, nl):
            total = total + decode(buf_q[t, k - 1], buf_s[t, k - 1])
        all_q[t, li], all_s[t, li] = code(total)
        for k in range(nl - 1):
            for copy in ra_copies(t, k, li):
                copy.start()

    def region_gather(t):
        settle(all_s.at[t, others_l], r_ra.at[0, t])
        settle(all_q.at[t, others_l], r_ra.at[1, t])

    def counts():
        n = jnp.zeros((n_reg, 1), F32)
        for i in range(nl):
            n = n + jnp.sum(onehot_t(pri[i]), axis=1, keepdims=True)
        return n + 1.0

    def region_force(t, i, get_v, n):
        s = jnp.concatenate(
            [decode(all_q[t, o, :, cols(i)], all_s[t, o]) for o in range(nl)], axis=0
        )
        return PREC * (s - n * get_v(i))

    def wait_rest():
        fetch(3).wait()
        fetch(5).wait()

    def pool_update():
        fetch(7).wait()
        for i in range(n_cols):
            e = step_cols(i)
            m = wide(pool_m, i) + (0.5 * e) * (lik_cols(i) - dev[:, cols(i)])
            pool_m1[:, cols(i)] = m
            pools_1[:, cols(i)] = wide(pools, i) + e * m

    def region_next():
        fetch(8).wait()
        region_gather(0)
        settle(pri.at[others_l], r_pr)
        n = counts()
        for i in range(n_cols):
            e = step_cols(i)
            g = region_force(0, i, lambda i: wide(regions, i), n)
            m = wide(region_m, i) + (0.5 * e) * g
            region_m1[:, cols(i)] = m
            regions_1[:, cols(i)] = wide(regions, i) + e * m
        deviation(lambda i: pools_1[:, cols(i)], lambda i: regions_1[:, cols(i)])

    def region_last():
        region_gather(1)
        n = counts()
        for i in range(n_cols):
            g = region_force(1, i, lambda i: regions_1[:, cols(i)], n)
            region_m1[:, cols(i)] += (0.5 * step_cols(i)) * g

    def pool_last():
        for i in range(n_cols):
            pool_m1[:, cols(i)] += (0.5 * step_cols(i)) * (lik_cols(i) - dev[:, cols(i)])

    def step_rows():
        chain = lax.broadcasted_iota(jnp.int32, (chains, 1), 0)
        e = jnp.zeros((chains, 1), F32)
        for c in range(chains):
            e = jnp.where(chain == c, step_s[c], e)
        return e

    def beta_next():
        fetch(9).wait()
        e = step_rows()
        m = beta_m[...] + (0.5 * e) * (population_sum(0) - total_feats * beta[...])
        beta_mn[...] = m
        beta_n[...] = beta[...] + e * m

    def beta_last():
        beta_mn[...] += (0.5 * step_rows()) * (population_sum(1) - total_feats * beta_n[...])

    def sum_next():
        region_sum(1, lambda i: pools_1[:, cols(i)])
        region_send(1)

    def sent():
        settle(line_s.at[:, others_f], s_lx.at[0])
        settle(line_q.at[:, others_f], s_lx.at[1])
        settle(xt_s.at[:, others_l], s_xt.at[0])
        settle(xt_q.at[:, others_l], s_xt.at[1])
        settle(buf_s, s_rr.at[0])
        settle(buf_q, s_rr.at[1])
        settle(all_s.at[:, others_l], s_ra.at[0])
        settle(all_q.at[:, others_l], s_ra.at[1])
        settle(pri.at[others_l], s_pr)

    def unpack(src, dst):
        for c in range(chains):
            dst[c] = src[:, pl.ds(c * g_own, g_own)]

    prologue()
    start_rows()
    slopes_first()
    logits_first()
    region_first()
    deviation_first()
    wait_rest()
    for j in range(nf - 1):
        residuals(0, j)
        likelihood(j)
    residuals(0, nf - 1)
    population_send(0)
    likelihood(nf - 1)
    pool_update()
    slopes_next()
    terms_next()
    sum_next()
    for j in range(nf):
        flip(j)
    beta_next()
    logits_next()
    region_reduce(0)
    unpack(pools_1, pools_n)
    region_reduce(1)
    residuals_all(1)
    population_send(1)
    for j in range(nf):
        likelihood(j)
    region_next()
    unpack(regions_1, regions_n)
    pool_last()
    unpack(pool_m1, pool_mn)
    region_last()
    unpack(region_m1, region_mn)
    beta_last()
    sent()


def emit(*refs):
    n = len(refs) // 2
    copies = [
        pltpu.make_async_copy(refs[i], refs[n + i], refs[-1].at[i]) for i in range(n)
    ]
    for copy in copies:
        copy.start()
    for copy in copies:
        copy.wait()


def body(
    nf,
    nl,
    design,
    labels,
    pool_ids,
    pool_region_index,
    step_size,
    beta,
    pools,
    regions,
    beta_momentum,
    pool_momentum,
    region_momentum,
):
    loans, feats = design.shape
    chains, owned, g_own = pools.shape
    n_reg = regions.shape[1]
    width = loans // nf
    lanes = chains * g_own
    nb = blocks_of(owned, g_own)
    prow = owned // nb
    rows = n_reg // nl
    vmem = pl.BlockSpec(memory_space=pltpu.VMEM)
    hbm = pl.BlockSpec(memory_space=pltpu.HBM)
    dma = pltpu.SemaphoreType.DMA
    args = (
        design,
        labels.reshape(nf, 1, width),
        pool_ids.reshape(nf, 1, width),
        pool_region_index.reshape(1, owned),
        step_size,
        beta,
        pools,
        regions,
        beta_momentum,
        pool_momentum,
        region_momentum,
    )
    outs = (beta, pools, regions, beta_momentum, pool_momentum, region_momentum)
    results = pl.pallas_call(
        functools.partial(kernel, nf, nl),
        out_shape=tuple(pltpu.VMEM(x.shape, F32) for x in outs),
        in_specs=[hbm] * len(args),
        out_specs=tuple(vmem for _ in outs),
        scratch_shapes=[
            pltpu.VMEM((owned, lanes), F32),
            pltpu.VMEM((n_reg, lanes), F32),
            pltpu.VMEM((owned, lanes), F32),
            pltpu.VMEM((n_reg, lanes), F32),
            pltpu.VMEM((nl, rows, lanes), F32),
            pltpu.VMEM((nf, width, feats), BF16),
            pltpu.VMEM((nf, 1, width), jnp.int32),
            pltpu.VMEM((nf, 1, width), jnp.int32),
            pltpu.VMEM((nl, 1, owned), jnp.int32),
            pltpu.SMEM(step_size.shape, F32),
            pltpu.VMEM(beta.shape, F32),
            pltpu.VMEM(pools.shape, F32),
            pltpu.VMEM(regions.shape, F32),
            pltpu.VMEM(beta.shape, F32),
            pltpu.VMEM(pools.shape, F32),
            pltpu.VMEM(regions.shape, F32),
            pltpu.VMEM((chains + g_own * min(256, feats) // feats, feats), BF16),
            pltpu.VMEM((nf, prow, width), F32),
            pltpu.VMEM((nf, nb * g_own, width), BF16),
            pltpu.VMEM((2 * chains * prow, nb * g_own), BF16),
            pltpu.VMEM((chains * prow, nb * g_own), F32),
            pltpu.VMEM((nf, chains, width), F32),
            pltpu.VMEM((owned, lanes), F32),
            pltpu.VMEM((2, nf, chains, width), F32),
            pltpu.VMEM((2, nf, nf, chains, width), I16),
            pltpu.VMEM((2, nf, nf, 1, width), F32),
            pltpu.VMEM((nf, chains, width), F32),
            pltpu.VMEM((chains, feats), F32),
            pltpu.VMEM((2, nl, chains, feats), I16),
            pltpu.VMEM((2, nl, 1, min(128, feats)), F32),
            pltpu.VMEM((2, nl, rows, lanes), I16),
            pltpu.VMEM((2, nl, 1, min(128, lanes)), F32),
            pltpu.VMEM((2, nl - 1, rows, lanes), I16),
            pltpu.VMEM((2, nl - 1, 1, min(128, lanes)), F32),
            pltpu.VMEM((2, nl, rows, lanes), I16),
            pltpu.VMEM((2, nl, 1, min(128, lanes)), F32),
            pltpu.VMEM((nf, feats, width), BF16),
            pltpu.VMEM((min(256, feats),) * 2, BF16),
            dma((10,)),
            dma((nf,)),
            dma((2,)),
            dma((2, 2, nf)),
            dma((2,)),
            dma((2, 2)),
            dma((2,)),
            dma((2, 2)),
            dma((2,)),
            dma((2, 2)),
            dma,
            dma,
        ],
        compiler_params=pltpu.CompilerParams(
            collective_id=0, has_side_effects=True, vmem_limit_bytes=VLIM << 20
        ),
    )(*[pltpu.with_memory_space_constraint(x, pltpu.HBM) for x in args])
    return pl.pallas_call(
        emit,
        out_shape=tuple(jax.ShapeDtypeStruct(x.shape, x.dtype) for x in outs),
        in_specs=[vmem] * len(outs),
        out_specs=tuple(hbm for _ in outs),
        scratch_shapes=[dma((len(outs),))],
        compiler_params=pltpu.CompilerParams(vmem_limit_bytes=16 << 20),
    )(*results)


VLIM = 30


def solution(mesh):
    in_specs = (
        P(("grp", "loan"), "feat"),
        P(("grp", "loan")),
        P(("grp", "loan")),
        P(("grp", "loan")),
        P("grp"),
        P("grp", "feat"),
        P("grp", "loan", "feat"),
        P("grp", None, "feat"),
        P("grp", "feat"),
        P("grp", "loan", "feat"),
        P("grp", None, "feat"),
    )
    out_specs = (
        P("grp", "feat"),
        P("grp", "loan", "feat"),
        P("grp", None, "feat"),
        P("grp", "feat"),
        P("grp", "loan", "feat"),
        P("grp", None, "feat"),
    )
    step = functools.partial(body, mesh.shape["feat"], mesh.shape["loan"])
    return jax.shard_map(step, mesh=mesh, in_specs=in_specs, out_specs=out_specs, check_vma=False)
```

```python
import functools

import jax
import jax.numpy as jnp
from jax import lax
from jax.experimental import pallas as pl
from jax.experimental.pallas import tpu as pltpu
from jax.sharding import PartitionSpec as P

PREC = 256.0
MESH = pl.DeviceIdType.MESH
NT = (((1,), (1,)), ((), ()))
NN = (((1,), (0,)), ((), ()))
F32 = jnp.float32
BF16 = jnp.bfloat16
I16 = jnp.int16
TOP = 32767.0


def dot(a, b, dims=NN):
    return lax.dot_general(a, b, dims, preferred_element_type=F32)


def halves(x):
    hi = x.astype(BF16)
    return hi, (x - hi.astype(F32)).astype(BF16)


def code(x):
    unit = min(128, x.shape[1])
    pieces = [x[:, i : i + unit] for i in range(0, x.shape[1], unit)]
    top = functools.reduce(jnp.maximum, [jnp.abs(p) for p in pieces])
    top = jnp.maximum(jnp.max(top, axis=0, keepdims=True), 1e-30)
    up = TOP / top
    q = jnp.concatenate([jnp.round(p * up).astype(jnp.int32).astype(I16) for p in pieces], axis=1)
    return q, top * (1.0 / TOP)


def code_cols(x):
    top = jnp.maximum(jnp.max(jnp.abs(x), axis=0, keepdims=True), 1e-30)
    return jnp.round(x * (TOP / top)).astype(jnp.int32).astype(I16), top * (1.0 / TOP)


def decode(q, scale):
    unit = scale.shape[1]
    return jnp.concatenate(
        [
            q[:, i : i + unit].astype(jnp.int32).astype(F32) * scale
            for i in range(0, q.shape[1], unit)
        ],
        axis=1,
    )


def blocks_of(owned, g_own):
    return max(1, min(256 // g_own, owned // 16))


def kernel(
    nf,
    nl,
    design_hbm,
    labels_hbm,
    ids_hbm,
    pri_hbm,
    step_hbm,
    beta_hbm,
    pools_hbm,
    regions_hbm,
    beta_m_hbm,
    pool_m_hbm,
    region_m_hbm,
    beta_n,
    pools_n,
    regions_n,
    beta_mn,
    pool_mn,
    region_mn,
    pools_1,
    regions_1,
    pool_m1,
    region_m1,
    sums,
    design,
    labels,
    ids,
    pri,
    step_s,
    beta,
    pools,
    regions,
    beta_m,
    pool_m,
    region_m,
    lhs,
    mask,
    fold,
    u4,
    lik,
    term,
    dev,
    part,
    line_q,
    line_s,
    resid_f,
    xt_f,
    xt_q,
    xt_s,
    part_q,
    part_s,
    buf_q,
    buf_s,
    all_q,
    all_s,
    flipped,
    eye,
    load,
    load_d,
    s_lx,
    r_lx,
    s_xt,
    r_xt,
    s_rr,
    r_rr,
    s_ra,
    r_ra,
    s_pr,
    r_pr,
):
    fi = lax.axis_index("feat")
    li = lax.axis_index("loan")
    chains, owned, g_own = pools.shape
    feats = beta.shape[1]
    n_reg = regions.shape[1]
    width = labels.shape[2]
    stride = feats // g_own
    total_feats = float(feats * nf)
    nb = blocks_of(owned, g_own)
    prow = owned // nb
    lanes = chains * g_own
    side = max(1, 128 // g_own)
    span = side * g_own
    nx = nf // 2

    def peer_of(k):
        return lax.rem(fi // 2 + k // 2, nx) * 2 + lax.rem(fi + k, 2)

    def each(n, act):
        if n <= 4:
            for k in range(n - 1, 0, -1):
                act(k)
        else:

            def step(k, carry):
                act(k)
                return carry

            lax.fori_loop(1, n, step, 0)

    def fetch_rows(j):
        return pltpu.make_async_copy(
            design_hbm.at[pl.ds(j * width, width), :],
            design.at[j],
            load_d.at[j],
        )

    def fetch(i):
        src, dst = (
            (beta_hbm, beta),
            (ids_hbm, ids),
            (pools_hbm, pools),
            (labels_hbm, labels),
            (pri_hbm, pri.at[li]),
            (step_hbm, step_s),
            (regions_hbm, regions),
            (pool_m_hbm, pool_m),
            (region_m_hbm, region_m),
            (beta_m_hbm, beta_m),
        )[i]
        return pltpu.make_async_copy(src, dst, load.at[i])

    barrier = pltpu.get_barrier_semaphore()
    for k in range(nl - 1, 0, -1):
        pl.semaphore_signal(
            barrier, inc=1, device_id={"loan": lax.rem(li + k, nl)}, device_id_type=MESH
        )
    each(
        nf,
        lambda k: pl.semaphore_signal(
            barrier, inc=1, device_id={"feat": peer_of(k)}, device_id_type=MESH
        ),
    )

    for i in range(2):
        fetch(i).start()
    fetch_rows(0).start()
    fetch(2).start()
    fetch_rows(1).start()

    def remote(src, dst, ss, rs, axis, peer):
        return pltpu.make_async_remote_copy(
            src_ref=src,
            dst_ref=dst,
            send_sem=ss,
            recv_sem=rs,
            device_id={axis: peer},
            device_id_type=MESH,
        )

    batch = (1, 1)

    def line_copies(t, k, j):
        some = pl.ds(j, batch[t])
        return [
            remote(
                ref.at[t, 0, some],
                ref.at[t, k, some],
                s_lx.at[i],
                r_lx.at[i, t, j],
                "feat",
                peer_of(k),
            )
            for i, ref in enumerate((line_s, line_q))
        ]

    def line_send(t, j, x):
        part[t, j] = x
        line_q[t, 0, j], line_s[t, 0, j] = code_cols(x)
        if t == 0 and j == 0:
            pl.semaphore_wait(barrier, nf + nl - 2)

        last = j - batch[t] + 1

        def go(k):
            for copy in line_copies(t, k, last):
                copy.start()

        if last % batch[t] == 0:
            each(nf, go)

    def settle(view, sem):
        pltpu.make_async_copy(view, view, sem).wait()

    others_f, others_l = pl.ds(1, nf - 1), pl.ds(1, nl - 1)

    def loan_peer(i):
        right = li // ((nl + 1) // 2)
        place = li * (1 - right) + (nl - 1 - li) * right
        far = nl - 1 - i - (place + 1 + i) // nl
        return far * (1 - right) + (nl - 1 - far) * right

    def loan_slot(peer):
        return lax.rem(peer - li + nl, nl)

    def xt_copies(t, k):
        peer = loan_peer(k)
        return [
            remote(
                ref.at[t, 0],
                ref.at[t, loan_slot(peer)],
                s_xt.at[i],
                r_xt.at[i, t],
                "loan",
                peer,
            )
            for i, ref in enumerate((xt_s, xt_q))
        ]

    def rr_copies(t, k):
        peer = loan_peer(k)
        return [
            remote(
                src.at[t, peer],
                dst.at[t, loan_slot(peer) - 1],
                s_rr.at[i],
                r_rr.at[i, t],
                "loan",
                peer,
            )
            for i, (src, dst) in enumerate(((part_s, buf_s), (part_q, buf_q)))
        ]

    def ra_copies(t, k, owner):
        return [
            remote(
                ref.at[t, owner],
                ref.at[t, owner],
                s_ra.at[i],
                r_ra.at[i, t],
                "loan",
                loan_peer(k),
            )
            for i, ref in enumerate((all_s, all_q))
        ]

    def pr_copy(k, owner):
        return remote(
            pri.at[owner], pri.at[owner], s_pr, r_pr, "loan", loan_peer(k)
        )

    def onehot_t(row):
        return (row == lax.broadcasted_iota(jnp.int32, (n_reg, owned), 0)).astype(F32)

    def wide(ref, i):
        return jnp.concatenate([ref[i * side + c] for c in range(side)], axis=1)

    def cols(i):
        return pl.ds(i * span, span)

    n_cols = lanes // span

    def prologue():
        size = eye.shape[0]
        tile = size // stride
        pick = (
            (
                lax.broadcasted_iota(jnp.int32, (tile, size), 1)
                == stride * lax.broadcasted_iota(jnp.int32, (tile, size), 0)
            )
            .astype(F32)
            .astype(BF16)
        )
        for i in range(feats // size):
            lhs[pl.ds(chains, tile), pl.ds(i * size, size)] = pick
        eye[...] = (
            (
                lax.broadcasted_iota(jnp.int32, (size, size), 0)
                == lax.broadcasted_iota(jnp.int32, (size, size), 1)
            )
            .astype(F32)
            .astype(BF16)
        )

    def start_rows():
        fetch(0).wait()
        for j in range(2, nf):
            fetch_rows(j).start()
        lhs[pl.ds(0, chains), :] = beta[...].astype(BF16)
        fetch(1).wait()

    def put_u4(c, blocks):
        hi, lo = halves(jnp.concatenate(blocks, axis=1))
        u4[pl.ds(c * prow, prow), :] = hi
        u4[pl.ds((chains + c) * prow, prow), :] = lo

    def slopes_first():
        fetch(2).wait()
        for c in range(chains):
            put_u4(c, [pools[c, pl.ds(k * prow, prow), :] for k in range(nb)])

    def slopes_next():
        for c in range(chains):
            put_u4(
                c,
                [
                    pools_1[pl.ds(k * prow, prow), pl.ds(c * g_own, g_own)]
                    for k in range(nb)
                ],
            )

    def pool_term(j):
        z = dot(u4[...], fold[j])
        m = mask[j]
        low = chains * prow
        for c in range(chains):
            a = z[c * prow : (c + 1) * prow] + z[low + c * prow : low + (c + 1) * prow]
            term[j, pl.ds(c, 1), :] = jnp.sum(a * m, axis=0, keepdims=True)

    first = li * owned

    turned = 2

    def sweep(j):
        fetch_rows(j).wait()
        size = eye.shape[0]
        line, slope = None, []
        for i in range(feats // size):
            depth = pl.ds(i * size, size)
            if i % 2 == 1 and i // 2 < turned or i == 0 and turned > 2:
                flipped[j, depth, :] = design[j, :, depth].T
                x = dot(lhs[:, depth], flipped[j, depth, :])
            else:
                x = dot(lhs[:, depth], design[j, :, depth], NT)
            line = x[:chains] if line is None else line + x[:chains]
            slope.append(x[chains:])
        local = ids[j] - first
        block = local // prow
        mask[j] = (
            local - block * prow == lax.broadcasted_iota(jnp.int32, (prow, width), 0)
        ).astype(F32)
        slope = jnp.concatenate(slope, axis=0)
        for b in range(nb):
            fold[j, pl.ds(b * g_own, g_own), :] = jnp.where(block == b, slope, 0.0).astype(BF16)
        part[0, j] = line

    def logits_first():
        sweep(0)
        for j in range(nf):
            if j + 1 < nf:
                sweep(j + 1)
            pool_term(j)
            line_send(0, j, term[j] + part[0, j])
            if j == 0:
                for i in (3, 4, 5, 6, 7, 8, 9):
                    fetch(i).start()

    def terms_next():
        for j in range(nf):
            pool_term(j)

    def flip(j):
        size = eye.shape[0]
        for i in range(feats // size):
            if i % 2 == 1 and i // 2 < turned or i == 0 and turned > 2:
                continue
            x = dot(eye[...], design[j, :, pl.ds(i * size, size)], NT)
            flipped[j, pl.ds(i * size, size), :] = x.astype(BF16)

    def logits_next():
        b16 = beta_n[...].astype(BF16)
        for j in range(nf):
            line_send(1, j, term[j] + dot(b16, flipped[j]))

    def residual(t, j):
        if j % batch[t] == 0:
            some = pl.ds(j, batch[t])
            settle(line_s.at[t, others_f, some], r_lx.at[0, t, j])
            settle(line_q.at[t, others_f, some], r_lx.at[1, t, j])

        def add(k, logit):
            return logit + line_q[t, k, j].astype(jnp.int32).astype(F32) * line_s[t, k, j]

        logit = part[t, j]
        if nf <= 4:
            for k in range(1, nf):
                logit = add(k, logit)
        else:
            logit = lax.fori_loop(1, nf, add, logit)
        mine = (labels[j].astype(F32) - jax.nn.sigmoid(logit)).astype(BF16)
        resid_f[j] = mine.astype(F32)
        return mine

    def residuals(t, j):
        x = dot(residual(t, j), design[j])
        if j == 0:
            xt_f[...] = x
        elif j != nf - 1:
            xt_f[...] += x
        else:
            xt_q[t, 0], xt_s[t, 0] = code(xt_f[...] + x)

    def residuals_all(t):
        half = batch[t]
        for i in range(0, nf, half):
            mine = [residual(t, j) for j in range(i, i + half)]
            x = dot(mine[0], design[i])
            for j in range(1, half):
                x = x + dot(mine[j], design[i + j])
            if i == 0:
                xt_f[...] = x
            elif i + half < nf:
                xt_f[...] += x
            else:
                xt_q[t, 0], xt_s[t, 0] = code(xt_f[...] + x)

    def population_send(t):
        for k in range(nl - 1):
            for copy in xt_copies(t, k):
                copy.start()

    def population_sum(t):
        settle(xt_s.at[t, others_l], r_xt.at[0, t])
        settle(xt_q.at[t, others_l], r_xt.at[1, t])
        total = decode(xt_q[t, li], xt_s[t, li])
        for j in range(1, nl):
            slot = lax.rem(li + nl - j, nl)
            total = total + decode(xt_q[t, slot], xt_s[t, slot])
        return total

    def likelihood(j):
        m = mask[j]
        a = jnp.concatenate(
            [(resid_f[j, pl.ds(c, 1), :] * m).astype(BF16) for c in range(chains)], axis=0
        )
        x = dot(a, fold[j], NT)
        if j == 0:
            lik[...] = x
        else:
            lik[...] += x

    def lik_cols(i):
        return jnp.concatenate(
            [
                jnp.concatenate(
                    [
                        lik[
                            pl.ds((i * side + c) * prow, prow), pl.ds(k * g_own, g_own)
                        ]
                        for c in range(side)
                    ],
                    axis=1,
                )
                for k in range(nb)
            ],
            axis=0,
        )

    def step_cols(i):
        lane = lax.broadcasted_iota(jnp.int32, (1, span), 1) // g_own
        e = jnp.zeros((1, span), F32)
        for c in range(side):
            e = jnp.where(lane == c, step_s[i * side + c], e)
        return e

    def region_sum(t, get):
        oht = onehot_t(pri[li])
        oht2 = jnp.concatenate([oht, oht], axis=1).astype(BF16)
        rows = n_reg // nl
        for i in range(n_cols):
            hi, lo = halves(get(i))
            sums[:, :, cols(i)] = dot(oht2, jnp.concatenate([hi, lo], axis=0)).reshape(
                nl, rows, span
            )
        for o in range(nl):
            part_q[t, o], part_s[t, o] = code(sums[o])

    def region_send(t):
        for k in range(nl - 1):
            for copy in rr_copies(t, k):
                copy.start()

    def deviation(get_u, get_v):
        oht = onehot_t(pri[li])
        eye = (
            lax.broadcasted_iota(jnp.int32, (owned, owned), 0)
            == lax.broadcasted_iota(jnp.int32, (owned, owned), 1)
        ).astype(F32)
        oh = dot(eye.astype(BF16), oht.astype(BF16), NT)
        oh2 = jnp.concatenate([oh, oh], axis=1).astype(BF16)
        for i in range(n_cols):
            hi, lo = halves(get_v(i))
            dev[:, cols(i)] = PREC * (get_u(i) - dot(oh2, jnp.concatenate([hi, lo], axis=0)))

    def region_first():
        fetch(4).wait()
        region_sum(0, lambda i: wide(pools, i))
        for k in range(nl - 1):
            pr_copy(k, li).start()
        region_send(0)

    def deviation_first():
        fetch(6).wait()
        deviation(lambda i: wide(pools, i), lambda i: wide(regions, i))

    def region_reduce(t):
        settle(buf_s.at[t], r_rr.at[0, t])
        settle(buf_q.at[t], r_rr.at[1, t])
        total = decode(part_q[t, li], part_s[t, li])
        for k in range(1, nl):
            total = total + decode(buf_q[t, k - 1], buf_s[t, k - 1])
        all_q[t, li], all_s[t, li] = code(total)
        for k in range(nl - 1):
            for copy in ra_copies(t, k, li):
                copy.start()

    def region_gather(t):
        settle(all_s.at[t, others_l], r_ra.at[0, t])
        settle(all_q.at[t, others_l], r_ra.at[1, t])

    def counts():
        n = jnp.zeros((n_reg, 1), F32)
        for i in range(nl):
            n = n + jnp.sum(onehot_t(pri[i]), axis=1, keepdims=True)
        return n + 1.0

    def region_force(t, i, get_v, n):
        s = jnp.concatenate(
            [decode(all_q[t, o, :, cols(i)], all_s[t, o]) for o in range(nl)], axis=0
        )
        return PREC * (s - n * get_v(i))

    def wait_rest():
        fetch(3).wait()
        fetch(5).wait()

    def pool_update():
        fetch(7).wait()
        for i in range(n_cols):
            e = step_cols(i)
            m = wide(pool_m, i) + (0.5 * e) * (lik_cols(i) - dev[:, cols(i)])
            pool_m1[:, cols(i)] = m
            pools_1[:, cols(i)] = wide(pools, i) + e * m

    def region_next():
        fetch(8).wait()
        region_gather(0)
        settle(pri.at[others_l], r_pr)
        n = counts()
        for i in range(n_cols):
            e = step_cols(i)
            g = region_force(0, i, lambda i: wide(regions, i), n)
            m = wide(region_m, i) + (0.5 * e) * g
            region_m1[:, cols(i)] = m
            regions_1[:, cols(i)] = wide(regions, i) + e * m
        deviation(lambda i: pools_1[:, cols(i)], lambda i: regions_1[:, cols(i)])

    def region_last():
        region_gather(1)
        n = counts()
        for i in range(n_cols):
            g = region_force(1, i, lambda i: regions_1[:, cols(i)], n)
            region_m1[:, cols(i)] += (0.5 * step_cols(i)) * g

    def pool_last():
        for i in range(n_cols):
            pool_m1[:, cols(i)] += (0.5 * step_cols(i)) * (lik_cols(i) - dev[:, cols(i)])

    def step_rows():
        chain = lax.broadcasted_iota(jnp.int32, (chains, 1), 0)
        e = jnp.zeros((chains, 1), F32)
        for c in range(chains):
            e = jnp.where(chain == c, step_s[c], e)
        return e

    def beta_next():
        fetch(9).wait()
        e = step_rows()
        m = beta_m[...] + (0.5 * e) * (population_sum(0) - total_feats * beta[...])
        beta_mn[...] = m
        beta_n[...] = beta[...] + e * m

    def beta_last():
        beta_mn[...] += (0.5 * step_rows()) * (population_sum(1) - total_feats * beta_n[...])

    def sum_next():
        region_sum(1, lambda i: pools_1[:, cols(i)])
        region_send(1)

    def sent():
        settle(line_s.at[:, others_f], s_lx.at[0])
        settle(line_q.at[:, others_f], s_lx.at[1])
        settle(xt_s.at[:, others_l], s_xt.at[0])
        settle(xt_q.at[:, others_l], s_xt.at[1])
        settle(buf_s, s_rr.at[0])
        settle(buf_q, s_rr.at[1])
        settle(all_s.at[:, others_l], s_ra.at[0])
        settle(all_q.at[:, others_l], s_ra.at[1])
        settle(pri.at[others_l], s_pr)

    def unpack(src, dst):
        for c in range(chains):
            dst[c] = src[:, pl.ds(c * g_own, g_own)]

    prologue()
    start_rows()
    slopes_first()
    logits_first()
    region_first()
    deviation_first()
    wait_rest()
    for j in range(nf - 1):
        residuals(0, j)
        likelihood(j)
    residuals(0, nf - 1)
    population_send(0)
    likelihood(nf - 1)
    pool_update()
    slopes_next()
    terms_next()
    sum_next()
    for j in range(nf):
        flip(j)
    region_reduce(0)
    beta_next()
    logits_next()
    unpack(pools_1, pools_n)
    region_reduce(1)
    residuals_all(1)
    population_send(1)
    for j in range(nf):
        likelihood(j)
    region_next()
    unpack(regions_1, regions_n)
    pool_last()
    unpack(pool_m1, pool_mn)
    region_last()
    unpack(region_m1, region_mn)
    beta_last()
    sent()


def emit(*refs):
    n = len(refs) // 2
    copies = [
        pltpu.make_async_copy(refs[i], refs[n + i], refs[-1].at[i]) for i in range(n)
    ]
    for copy in copies:
        copy.start()
    for copy in copies:
        copy.wait()


def body(
    nf,
    nl,
    design,
    labels,
    pool_ids,
    pool_region_index,
    step_size,
    beta,
    pools,
    regions,
    beta_momentum,
    pool_momentum,
    region_momentum,
):
    loans, feats = design.shape
    chains, owned, g_own = pools.shape
    n_reg = regions.shape[1]
    width = loans // nf
    lanes = chains * g_own
    nb = blocks_of(owned, g_own)
    prow = owned // nb
    rows = n_reg // nl
    vmem = pl.BlockSpec(memory_space=pltpu.VMEM)
    hbm = pl.BlockSpec(memory_space=pltpu.HBM)
    dma = pltpu.SemaphoreType.DMA
    args = (
        design,
        labels.reshape(nf, 1, width),
        pool_ids.reshape(nf, 1, width),
        pool_region_index.reshape(1, owned),
        step_size,
        beta,
        pools,
        regions,
        beta_momentum,
        pool_momentum,
        region_momentum,
    )
    outs = (beta, pools, regions, beta_momentum, pool_momentum, region_momentum)
    results = pl.pallas_call(
        functools.partial(kernel, nf, nl),
        out_shape=tuple(pltpu.VMEM(x.shape, F32) for x in outs),
        in_specs=[hbm] * len(args),
        out_specs=tuple(vmem for _ in outs),
        scratch_shapes=[
            pltpu.VMEM((owned, lanes), F32),
            pltpu.VMEM((n_reg, lanes), F32),
            pltpu.VMEM((owned, lanes), F32),
            pltpu.VMEM((n_reg, lanes), F32),
            pltpu.VMEM((nl, rows, lanes), F32),
            pltpu.VMEM((nf, width, feats), BF16),
            pltpu.VMEM((nf, 1, width), jnp.int32),
            pltpu.VMEM((nf, 1, width), jnp.int32),
            pltpu.VMEM((nl, 1, owned), jnp.int32),
            pltpu.SMEM(step_size.shape, F32),
            pltpu.VMEM(beta.shape, F32),
            pltpu.VMEM(pools.shape, F32),
            pltpu.VMEM(regions.shape, F32),
            pltpu.VMEM(beta.shape, F32),
            pltpu.VMEM(pools.shape, F32),
            pltpu.VMEM(regions.shape, F32),
            pltpu.VMEM((chains + g_own * min(256, feats) // feats, feats), BF16),
            pltpu.VMEM((nf, prow, width), F32),
            pltpu.VMEM((nf, nb * g_own, width), BF16),
            pltpu.VMEM((2 * chains * prow, nb * g_own), BF16),
            pltpu.VMEM((chains * prow, nb * g_own), F32),
            pltpu.VMEM((nf, chains, width), F32),
            pltpu.VMEM((owned, lanes), F32),
            pltpu.VMEM((2, nf, chains, width), F32),
            pltpu.VMEM((2, nf, nf, chains, width), I16),
            pltpu.VMEM((2, nf, nf, 1, width), F32),
            pltpu.VMEM((nf, chains, width), F32),
            pltpu.VMEM((chains, feats), F32),
            pltpu.VMEM((2, nl, chains, feats), I16),
            pltpu.VMEM((2, nl, 1, min(128, feats)), F32),
            pltpu.VMEM((2, nl, rows, lanes), I16),
            pltpu.VMEM((2, nl, 1, min(128, lanes)), F32),
            pltpu.VMEM((2, nl - 1, rows, lanes), I16),
            pltpu.VMEM((2, nl - 1, 1, min(128, lanes)), F32),
            pltpu.VMEM((2, nl, rows, lanes), I16),
            pltpu.VMEM((2, nl, 1, min(128, lanes)), F32),
            pltpu.VMEM((nf, feats, width), BF16),
            pltpu.VMEM((min(256, feats),) * 2, BF16),
            dma((10,)),
            dma((nf,)),
            dma((2,)),
            dma((2, 2, nf)),
            dma((2,)),
            dma((2, 2)),
            dma((2,)),
            dma((2, 2)),
            dma((2,)),
            dma((2, 2)),
            dma,
            dma,
        ],
        compiler_params=pltpu.CompilerParams(
            collective_id=0, has_side_effects=True, vmem_limit_bytes=VLIM << 20
        ),
    )(*[pltpu.with_memory_space_constraint(x, pltpu.HBM) for x in args])
    return pl.pallas_call(
        emit,
        out_shape=tuple(jax.ShapeDtypeStruct(x.shape, x.dtype) for x in outs),
        in_specs=[vmem] * len(outs),
        out_specs=tuple(hbm for _ in outs),
        scratch_shapes=[dma((len(outs),))],
        compiler_params=pltpu.CompilerParams(vmem_limit_bytes=16 << 20),
    )(*results)


VLIM = 30


def solution(mesh):
    in_specs = (
        P(("grp", "loan"), "feat"),
        P(("grp", "loan")),
        P(("grp", "loan")),
        P(("grp", "loan")),
        P("grp"),
        P("grp", "feat"),
        P("grp", "loan", "feat"),
        P("grp", None, "feat"),
        P("grp", "feat"),
        P("grp", "loan", "feat"),
        P("grp", None, "feat"),
    )
    out_specs = (
        P("grp", "feat"),
        P("grp", "loan", "feat"),
        P("grp", None, "feat"),
        P("grp", "feat"),
        P("grp", "loan", "feat"),
        P("grp", None, "feat"),
    )
    step = functools.partial(body, mesh.shape["feat"], mesh.shape["loan"])
    return jax.shard_map(step, mesh=mesh, in_specs=in_specs, out_specs=out_specs, check_vma=False)
```
